32 devices in a mesh: sn: 8 (over z, x), rhs: 4 (over y, core).
Axes of the slice: x: 2, y: 2, z: 4, core: 2. Of those that a mesh axis runs over, the one named last changes fastest.
Arguments:
- right_side: float32 [15, 128, 2048], P(None, 'rhs', 'sn'), may hold values from -6 to 6
- inverse_diag: float32 [15, 2048, 2048], P(None, 'sn', 'rhs'), may hold values from -1 to 2
- factor_blocks: float32 [768, 128, 128], P('sn'), may hold values from -0.21875 to 0.21875
- parent: int32 [15], replicated, may hold values from 0 to 14, as said below
- node_order: int32 [15], replicated, may hold values from 1025 to 2048, as said below
- block_row: int32 [768], P('sn'), may hold values from 0 to 239, as said below
- block_col: int32 [768], P('sn'), may hold values from 0 to 223, as said below
Outputs:
- solution: float32 [15, 128, 2048], P(None, 'rhs', 'sn')
The draws below stay inside these ranges and needn't reach their ends.
Inputs may be any that keep to these rules, and one draw needn't show every extreme that they name: Nodes of level k have their parent on level k + 1, every node above level 0 has exactly two children, and the root, node 14, is its own parent. `node_order`: some supernode has order 2048. `block_row`: block index = node * 16 + block within the node. Block k is held by index k // 96 of sn. `block_col`: block index = node * 16 + block within the node; never a block of the root. `inverse_diag`: each supernode's inverse is lower triangular (zero above the diagonal).
All inputs are finite; a program needn't handle non-finite values.
Results may differ from the reference program's by a relative error of at most 0.00011.
Values sent between devices are 32-bit elements; how exact they have to be, the bound alone decides.
A program may use at most 128 MiB of HBM per device.

```python
import jax
import jax.numpy as jnp
from jax import lax

S = 2048
BS = 128
NB = 16
LEVELS = 4
NODES = 15
SCEN = 128
SLOTS = 768


def level_starts():
    layout = []
    offset_value = 0
    for level_index in range(LEVELS):
        members = 2 ** (LEVELS - 1 - level_index)
        layout.append((offset_value, members))
        offset_value += members
    return layout


def tree_and_slots(key):
    base_key = jax.random.fold_in(key, 11)
    layout = level_starts()
    pieces = []
    for level_index in range(LEVELS - 1):
        members = layout[level_index][1]
        shuffled = jax.random.permutation(jax.random.fold_in(base_key, level_index), members).astype(jnp.int32)
        pieces.append(layout[level_index + 1][0] + shuffled // 2)
    pieces.append(jnp.full((1,), NODES - 1, jnp.int32))
    parent = jnp.concatenate(pieces).astype(jnp.int32)
    col_block = jax.random.randint(jax.random.fold_in(base_key, 101), (SLOTS,), 0, (NODES - 1) * NB).astype(jnp.int32)
    col_node = col_block // NB
    col_level = jnp.zeros((SLOTS,), jnp.int32)
    for level_index in range(1, LEVELS):
        col_level = col_level + (col_node >= layout[level_index][0]).astype(jnp.int32)
    raw_steps = jax.random.randint(jax.random.fold_in(base_key, 102), (SLOTS,), 0, 1 << 20).astype(jnp.int32)
    steps_up = 1 + raw_steps % (LEVELS - 1 - col_level)
    walker = col_node
    for repeat in range(LEVELS - 1):
        walker = jnp.where(repeat < steps_up, jnp.take(parent, walker), walker)
    stray = jax.random.randint(jax.random.fold_in(base_key, 103), (SLOTS,), 0, 8) == 0
    stray_node = jax.random.randint(jax.random.fold_in(base_key, 104), (SLOTS,), 0, NODES).astype(jnp.int32)
    row_node = jnp.where(stray, stray_node, walker)
    inner_block = jax.random.randint(jax.random.fold_in(base_key, 105), (SLOTS,), 0, NB).astype(jnp.int32)
    row_block = (row_node * NB + inner_block).astype(jnp.int32)
    return (parent, row_block, col_block)


def draw_parent(key, part):
    return tree_and_slots(key)[0]


def draw_block_row(key, part):
    return tree_and_slots(key)[1]


def draw_block_col(key, part):
    return tree_and_slots(key)[2]


def draw_node_order(key, part):
    orders = S // 2 + 1 + jax.random.randint(jax.random.fold_in(key, 23), (NODES,), 0, S - S // 2)
    fullest = jax.random.randint(jax.random.fold_in(key, 24), (), 0, NODES)
    return jnp.where(jnp.arange(NODES) == fullest, S, orders).astype(jnp.int32)


def draw_inverse_diag(key, part):
    row_index = jnp.arange(S)[:, None]
    col_index = jnp.arange(S)[None, :]
    values = jax.random.uniform(jax.random.fold_in(key, 31), (NODES, S, S), jnp.float32, -1.0, 1.0)
    diagonal = 1.1 + 0.5 * values
    lower = values * (1.04 / S ** 0.5)
    return jnp.where(row_index == col_index, diagonal, jnp.where(row_index > col_index, lower, 0.0)).astype(jnp.float32)


def steps_of(rng, extent, cuts, smallest, top_value):
    def one(position, blocks):
        draws = jax.random.uniform(jax.random.fold_in(jax.random.fold_in(rng, 6), position), (blocks,), jnp.float32, smallest / len(cuts), top_value / len(cuts))
        return jnp.repeat(jnp.exp(draws), extent[position] // blocks).reshape((-1,) + (1,) * (len(extent) - position - 1))

    gain = one(*cuts[0])
    for cut in cuts[1:]:
        gain = gain * one(*cut)
    return gain


def gaussian(key, shape, deviation, bound, cuts=(), kind=jnp.bfloat16):
    result = jax.random.normal(key, shape, jnp.float32) * deviation
    if len(cuts) > 0:
        result = steps_of(key, shape, cuts, -0.22, 0.18) * result
    return jnp.clip(result, min=-bound, max=bound).astype(kind)


def setup_inputs(seed: int = 0) -> dict:
    key_of = jax.random.split(jax.random.key(seed), 8)
    right_side = gaussian(key_of[0], (NODES, SCEN, S), 1.0, 6.0, ((1, 4), (2, 8)), jnp.float32)
    inverse_diag = draw_inverse_diag(jax.random.fold_in(key_of[7], 71), 0)
    factor_blocks = gaussian(key_of[2], (SLOTS, BS, BS), (SLOTS * BS // ((NODES - 2 ** (LEVELS - 1)) * NB)) ** -0.5, 0.21875, ((0, 8),), jnp.float32)
    parent = draw_parent(jax.random.fold_in(key_of[7], 71), 0)
    node_order = draw_node_order(jax.random.fold_in(key_of[7], 71), 0)
    block_row = draw_block_row(jax.random.fold_in(key_of[7], 71), 0)
    block_col = draw_block_col(jax.random.fold_in(key_of[7], 71), 0)
    return {"right_side": right_side, "inverse_diag": inverse_diag, "factor_blocks": factor_blocks, "parent": parent, "node_order": node_order, "block_row": block_row, "block_col": block_col}


def level_layout():
    layout = []
    offset_value = 0
    for level_index in range(LEVELS):
        members = 2 ** (LEVELS - 1 - level_index)
        layout.append((offset_value, members))
        offset_value += members
    return layout


def to_blocks(values):
    count, scen_count, rows_total = values.shape
    return jnp.transpose(values.reshape(count, scen_count, NB, BS), (0, 2, 1, 3)).reshape(count * NB, scen_count, BS)


def from_blocks(values):
    count = values.shape[0] // NB
    scen_count = values.shape[1]
    return jnp.transpose(values.reshape(count, NB, scen_count, BS), (0, 2, 1, 3)).reshape(count, scen_count, NB * BS)


def slot_validity(parent, block_row, block_col):
    col_node = block_col // NB
    row_node = block_row // NB
    walker = col_node
    valid = jnp.zeros(col_node.shape, dtype=bool)
    for repeat in range(LEVELS - 1):
        walker = jnp.take(parent, walker)
        valid = valid | (walker == row_node)
    col_level = jnp.zeros(col_node.shape, jnp.int32)
    layout = level_layout()
    for level_index in range(1, LEVELS):
        col_level = col_level + (col_node >= layout[level_index][0]).astype(jnp.int32)
    return valid, col_level


def reference(right_side, inverse_diag, factor_blocks, parent, node_order, block_row, block_col):
    valid, col_level = slot_validity(parent, block_row, block_col)
    live = (jnp.arange(S, dtype=jnp.int32)[None, :] < node_order[:, None]).astype(jnp.float32)
    partial_blocks = jnp.zeros((NODES * NB, SCEN, BS), jnp.float32)
    solved_blocks = jnp.zeros((NODES * NB, SCEN, BS), jnp.float32)
    layout = level_layout()
    for level_index in range(LEVELS):
        first_node, members = layout[level_index]
        stop_node = first_node + members
        partial_level = from_blocks(partial_blocks[first_node * NB:stop_node * NB])
        rhs_level = (right_side[first_node:stop_node] - partial_level) * live[first_node:stop_node, None, :]
        solved_level = jnp.einsum("ncj,nij->nci", rhs_level, inverse_diag[first_node:stop_node], precision=lax.Precision.HIGHEST)
        solved_level = solved_level * live[first_node:stop_node, None, :]
        solved_blocks = solved_blocks.at[first_node * NB:stop_node * NB].set(to_blocks(solved_level))
        if level_index < LEVELS - 1:
            weights = (valid & (col_level == level_index)).astype(jnp.float32)
            columns = jnp.take(solved_blocks, block_col, axis=0)
            update_terms = jnp.einsum("kij,kcj->kci", factor_blocks, columns, precision=lax.Precision.HIGHEST)
            update_terms = update_terms * weights[:, None, None]
            partial_blocks = partial_blocks.at[block_row].add(update_terms)
    return from_blocks(solved_blocks)
```

```python
import functools

import jax
import jax.numpy as jnp
from jax import lax
from jax.experimental import pallas as pl
from jax.experimental.pallas import tpu as pltpu
from jax.sharding import PartitionSpec as P

S = 2048
BS = 128
NB = 16
LEVELS = 4


def level_layout():
    layout = []
    offset_value = 0
    for level_index in range(LEVELS):
        members = 2 ** (LEVELS - 1 - level_index)
        layout.append((offset_value, members))
        offset_value += members
    return layout


def to_blocks(values):
    count, scen_count, rows_total = values.shape
    return jnp.transpose(values.reshape(count, scen_count, NB, BS), (0, 2, 1, 3)).reshape(
        count * NB, scen_count, BS
    )


def from_blocks(values):
    count = values.shape[0] // NB
    scen_count = values.shape[1]
    return jnp.transpose(values.reshape(count, NB, scen_count, BS), (0, 2, 1, 3)).reshape(
        count, scen_count, NB * BS
    )


def table_lookup(table, index_values):
    hits = index_values[:, None] == jnp.arange(table.shape[0], dtype=jnp.int32)[None, :]
    return jnp.sum(jnp.where(hits, table[None, :], 0), axis=1)


def per_device(right_side, inverse_diag, factor_blocks, parent, node_order, block_row, block_col):
    node_total, sc_dev, rows_s = right_side.shape
    layout = level_layout()
    col_node = block_col // NB
    row_node = block_row // NB
    walker = col_node
    valid = jnp.zeros(col_node.shape, dtype=bool)
    for repeat in range(LEVELS - 1):
        walker = table_lookup(parent, walker)
        valid = valid | (walker == row_node)
    col_level = jnp.zeros(col_node.shape, jnp.int32)
    for level_index in range(1, LEVELS):
        col_level = col_level + (col_node >= layout[level_index][0]).astype(jnp.int32)
    own_offset = lax.axis_index("sn") * rows_s
    live = (jnp.arange(S, dtype=jnp.int32)[None, :] < node_order[:, None]).astype(jnp.float32)
    own_rows = own_offset + jnp.arange(rows_s, dtype=jnp.int32)
    live_own = (own_rows[None, :] < node_order[:, None]).astype(jnp.float32)
    partial_blocks = jnp.zeros((node_total * NB, sc_dev, BS), jnp.float32)
    solved_blocks = jnp.zeros((node_total * NB, sc_dev, BS), jnp.float32)
    pieces_out = []
    for level_index in range(LEVELS):
        first_node, members = layout[level_index]
        stop_node = first_node + members
        placed = lax.dynamic_update_slice_in_dim(
            jnp.zeros((members, sc_dev, S), jnp.float32),
            right_side[first_node:stop_node],
            own_offset,
            2,
        )
        r_term = placed - from_blocks(partial_blocks[first_node * NB : stop_node * NB])
        r_full = lax.psum(r_term, "sn")
        masked = r_full * live[first_node:stop_node, None, :]
        moved = lax.all_to_all(masked, "rhs", split_axis=2, concat_axis=1, tiled=True)
        block_inverse = inverse_diag[first_node:stop_node]

        def inverse_term(offset, length, moved=moved, block_inverse=block_inverse):
            return jnp.einsum("ncj,nij->cni", moved, block_inverse, precision=lax.Precision.HIGHEST)

        summed = lax.psum_scatter(
            inverse_term(jnp.int32(0), sc_dev * lax.axis_size("rhs")),
            "rhs",
            scatter_dimension=0,
            tiled=True,
        )
        y_piece = jnp.transpose(summed, (1, 0, 2))
        y_piece = y_piece * live_own[first_node:stop_node, None, :]
        pieces_out.append(y_piece)
        if level_index < LEVELS - 1:
            gathered = lax.all_gather(y_piece, "sn", axis=2, tiled=True)
            solved_blocks = solved_blocks.at[first_node * NB : stop_node * NB].set(
                to_blocks(gathered)
            )
            weights = (valid & (col_level == level_index)).astype(jnp.float32)
            columns = lax.map(
                lambda block, source=solved_blocks: lax.dynamic_index_in_dim(
                    source, block, 0, keepdims=False
                ),
                block_col,
            )
            update_terms = jnp.einsum(
                "kij,kcj->kci", factor_blocks, columns, precision=lax.Precision.HIGHEST
            )
            update_terms = update_terms * weights[:, None, None]
            partial_blocks = partial_blocks.at[block_row].add(update_terms)
    return jnp.concatenate(pieces_out, axis=0)


def split(values):
    high = values.astype(jnp.bfloat16)
    low = (values - high.astype(jnp.float32)).astype(jnp.bfloat16)
    return high, low


def dot_nt(left, right):
    return lax.dot_general(
        left, right, (((1,), (1,)), ((), ())), preferred_element_type=jnp.float32
    )


def kernel(
    ns,
    nc,
    parent_s,
    order_s,
    col_s,
    rhs_ref,
    row_v,
    col_v,
    inv_hbm,
    fac_hbm,
    out_ref,
    *scratch,
):
    layout = level_layout()
    names = iter(scratch)
    inv_f, inv_h, inv_l, fac_f, fac_w, upd, sel, solved = [next(names) for _ in range(8)]
    own = [next(names) for _ in layout]
    held = [next(names) for _ in layout]
    stage = [next(names) for _ in layout]
    terms = [next(names) for _ in layout]
    part = [None] + [next(names) for _ in layout[1:]]
    got = [None] + [next(names) for _ in layout[1:]]
    load_sem = next(names)
    a_send, a_recv, b_send, b_recv, c_send, c_recv, d_send, d_recv = [
        next(names) for _ in range(8)
    ]

    r = lax.axis_index("sn")
    c = lax.axis_index("rhs")
    q = ns // nc
    group = r // q
    inner = r % q
    active = c <= group
    has_above = group < nc - 1
    has_below = group > 0
    beside = r + 1 - 2 * inner
    slots = fac_f.shape[0]
    sc = rhs_ref.shape[1]
    rows_s = rhs_ref.shape[2]
    hb = rows_s // BS
    low_nodes = layout[0][1]
    total = inv_f.shape[0]

    load_a = pltpu.make_async_copy(
        inv_hbm.at[pl.ds(0, low_nodes)], inv_f.at[pl.ds(0, low_nodes)], load_sem.at[0]
    )
    load_b = pltpu.make_async_copy(
        inv_hbm.at[pl.ds(low_nodes, total - low_nodes)],
        inv_f.at[pl.ds(low_nodes, total - low_nodes)],
        load_sem.at[1],
    )
    load_c = pltpu.make_async_copy(fac_hbm, fac_f, load_sem.at[2])
    load_a.start()
    load_b.start()
    load_c.start()

    barrier = pltpu.get_barrier_semaphore()
    for dr in range(ns):
        for dc in range(nc):
            if dr or dc:
                pl.semaphore_signal(
                    barrier,
                    inc=1,
                    device_id=(lax.rem(r + dr, ns), lax.rem(c + dc, nc)),
                    device_id_type=pl.DeviceIdType.MESH,
                )

    start_upper = low_nodes * NB

    @pl.loop(start_upper, solved.shape[0])
    def _(index):
        solved[index] = jnp.zeros((sc, BS), jnp.float32)

    def live_rows(node, h):
        lanes = lax.broadcasted_iota(jnp.int32, (sc, BS), 1) + (r * rows_s + h * BS)
        return lanes < order_s[node]

    def own_from(level):
        first, members = layout[level]

        @pl.loop(0, members)
        def _(n):
            for h in range(hb):
                value = rhs_ref[first + n, :, h * BS : (h + 1) * BS]
                if level:
                    value = value - part[level][r * (members * hb) + n * hb + h]
                    for d in range(1, ns):
                        value = value - got[level][lax.rem(r + d, ns), n * hb + h]
                own[level][n * hb + h] = jnp.where(live_rows(first + n, h), value, 0.0)

    pending = []

    def copy(src, dst, ssem, rsem, dev):
        return pltpu.make_async_remote_copy(
            src_ref=src,
            dst_ref=dst,
            send_sem=ssem,
            recv_sem=rsem,
            device_id=dev,
            device_id_type=pl.DeviceIdType.MESH,
        )

    def send(cond, make):
        def go():
            make().start()

        def done():
            make().wait_send()

        if cond is None:
            go()
        else:
            pl.when(cond)(go)
        pending.append((cond, done))

    def drain(copies):
        for cond, done in copies:
            if cond is None:
                done()
            else:
                pl.when(cond)(done)
        copies.clear()

    own_from(0)
    pl.semaphore_wait(barrier, ns * nc - 1)

    for level in range(LEVELS):
        first, members = layout[level]
        mh = members * hb
        base = first * NB

        if level:
            def one_block(k, carry):
                block = col_s[k]
                node = block // NB
                inside = block % NB
                offset = jnp.int32(0)
                count = jnp.int32(layout[0][1])
                for begin, many in layout[1:-1]:
                    above = node >= begin
                    offset = jnp.where(above, begin, offset)
                    count = jnp.where(above, many, count)
                index = (
                    offset * NB
                    + (inside // hb) * (count * hb)
                    + (node - offset) * hb
                    + inside % hb
                )
                high, low = split(solved[index])
                left = jnp.concatenate(
                    [
                        jnp.concatenate([high, high], axis=1),
                        jnp.concatenate([low, jnp.zeros_like(low)], axis=1),
                    ],
                    axis=0,
                )
                both = dot_nt(left, fac_w[k])
                upd[pl.ds(pl.multiple_of(k * sc, sc), sc), :] = both[:sc] + both[sc:]
                return carry

            lax.fori_loop(0, slots, one_block, 0, unroll=8)

            sel_first = (first - low_nodes) * NB
            picked = sel[sel_first : sel_first + members * NB, :]
            for s in range(0, sc, 2):
                pair = jnp.concatenate(
                    [upd[pl.ds(s + t, slots, stride=sc), :] for t in range(2)], axis=1
                )
                high, low = split(pair)
                summed = jnp.dot(
                    picked, high, preferred_element_type=jnp.float32
                ) + jnp.dot(picked, low, preferred_element_type=jnp.float32)
                for t in range(2):
                    part[level].reshape(members * NB * sc, BS)[
                        pl.ds(s + t, members * NB, stride=sc), :
                    ] = summed[:, t * BS : (t + 1) * BS]
            earlier = list(pending)
            pending.clear()
            for d in range(1, ns):
                to = lax.rem(r + d, ns)
                send(
                    None,
                    lambda to=to, d=d, level=level, mh=mh: copy(
                        part[level].at[pl.ds(to * mh, mh)],
                        got[level].at[r],
                        a_send.at[level, d],
                        a_recv.at[level, d],
                        (to, c),
                    ),
                )
            drain(earlier)
            for d in range(1, ns):
                src_r = lax.rem(r + d, ns)
                piece = got[level].at[src_r]
                copy(
                    piece, piece, a_send.at[level, d], a_recv.at[level, ns - d], (src_r, c)
                ).wait_recv()
            own_from(level)

        pieces = min(4, members)
        nodes = members // pieces
        size = nodes * hb

        def rows(ch, size=size):
            return pl.ds(ch * size, size)

        for ch in range(pieces):
            send(
                c != group,
                lambda ch=ch, level=level, rows=rows: copy(
                    own[level].at[rows(ch)],
                    held[level].at[inner * nc + c, rows(ch)],
                    b_send.at[level, 0, 0, ch],
                    b_recv.at[level, inner * nc + c, ch],
                    (r, group),
                ),
            )

        @pl.when(c == group)
        def _(level=level, mh=mh):
            @pl.loop(0, mh)
            def _(i):
                held[level][inner * nc + c, i] = own[level][i]

        def wait_held(cond, slot, ch, level=level, rows=rows):
            @pl.when(cond)
            def _():
                piece = held[level].at[slot, rows(ch)]
                copy(
                    piece,
                    piece,
                    b_send.at[level, 0, 0, ch],
                    b_recv.at[level, slot, ch],
                    (r, c),
                ).wait_recv()

        def forward(ch, level=level, rows=rows):
            for i in range(nc):
                c2 = lax.rem(c // 2 + i // 2, nc // 2) * 2 + lax.rem(c + i, 2)
                slot = inner * nc + c2
                wait_held(active if i else active & (c != group), slot, ch)
                for way, (cond, to) in enumerate([(active & has_above, r + q), (active, beside)]):
                    send(
                        cond,
                        lambda slot=slot, way=way, to=to, i=i: copy(
                            held[level].at[slot, rows(ch)],
                            held[level].at[slot, rows(ch)],
                            b_send.at[level, 1 + way, i, ch],
                            b_recv.at[level, slot, ch],
                            (to, c),
                        ),
                    )

        def product(ch, level=level, first=first, nodes=nodes, rows=rows):
            for c2 in range(nc):
                wait_held(active, (1 - inner) * nc + c2, ch)

            @pl.when(active)
            def _():
                @pl.loop(ch * nodes, (ch + 1) * nodes)
                def _(n):
                    columns = []
                    for qi in range(q):
                        for h in range(hb):
                            columns.append(
                                jnp.concatenate(
                                    [held[level][qi * nc + c2, n * hb + h] for c2 in range(nc)],
                                    axis=0,
                                )
                            )
                    left = jnp.concatenate(columns, axis=1)
                    high, low = split(left)
                    right_h = inv_h[first + n]
                    right_l = inv_l[first + n]
                    value = dot_nt(high, right_h) + (
                        dot_nt(low, right_h) + dot_nt(high, right_l)
                    )
                    for c2 in range(nc):
                        for h in range(hb):
                            stage[level][c2, n * hb + h] = value[
                                c2 * sc : (c2 + 1) * sc, h * BS : (h + 1) * BS
                            ]

            for d in range(1, nc):
                to = lax.rem(c + d, nc)
                send(
                    active,
                    lambda to=to, d=d: copy(
                        stage[level].at[to, rows(ch)],
                        terms[level].at[c, rows(ch)],
                        c_send.at[level, d, ch],
                        c_recv.at[level, c, ch],
                        (r, to),
                    ),
                )

        for ch in range(pieces + 1):
            if ch < pieces:
                forward(ch)
            if level == 0 and ch == 0:
                load_a.wait()

                @pl.when(active)
                def _():
                    split_inverse(inv_f, inv_h, inv_l, 0, low_nodes)

            if ch > 0:
                product(ch - 1)

        def store_at(i, value, level=level, base=base, mh=mh, first_term=False):
            solved_own = solved if level < LEVELS - 1 else part[level]
            spot = base + r * mh + i if level < LEVELS - 1 else r * mh + i
            solved_own[spot] = value if first_term else solved_own[spot] + value

        for c2 in range(nc):

            @pl.when((c2 <= group) & (c == c2))
            def _(c2=c2):
                @pl.loop(0, mh)
                def _(i):
                    store_at(i, stage[level][c2, i], first_term=c2 == 0)

            @pl.when((c2 <= group) & (c != c2))
            def _(c2=c2):
                for ch in range(pieces):
                    piece = terms[level].at[c2, rows(ch)]
                    copy(
                        piece, piece, c_send.at[level, 0, ch], c_recv.at[level, c2, ch], (r, c)
                    ).wait_recv()

                @pl.loop(0, mh)
                def _(i):
                    store_at(i, terms[level][c2, i], first_term=c2 == 0)

        @pl.loop(0, members)
        def _(n, level=level, first=first, base=base, mh=mh):
            for h in range(hb):
                i = n * hb + h
                solved_own = solved if level < LEVELS - 1 else part[level]
                spot = base + r * mh + i if level < LEVELS - 1 else r * mh + i
                value = jnp.where(live_rows(first + n, h), solved_own[spot], 0.0)
                out_ref[first + n, :, h * BS : (h + 1) * BS] = value
                if level < LEVELS - 1:
                    solved_own[spot] = value

        if level < LEVELS - 1:
            half = mh // 2
            used = iter(range(d_send.shape[1]))

            def rows_of(r0, p, base=base, mh=mh, half=half):
                return solved.at[pl.ds(base + r0 * mh + p * half, half)]

            def wait_rows(cond, r0, p, level=level, rows_of=rows_of):
                def go():
                    piece = rows_of(r0, p)
                    copy(
                        piece, piece, d_send.at[level, 0], d_recv.at[level, p, r0], (r, c)
                    ).wait_recv()

                go() if cond is None else pl.when(cond)(go)

            def pass_rows(cond, r0, p, to, level=level, used=used, rows_of=rows_of):
                place = next(used)
                send(
                    cond,
                    lambda: copy(
                        rows_of(r0, p),
                        rows_of(r0, p),
                        d_send.at[level, place],
                        d_recv.at[level, p, r0],
                        (to, c),
                    ),
                )

            for p in range(2):
                pass_rows(None, r, p, beside)
                pass_rows(has_above, r, p, r + q)
                pass_rows(has_below, r, p, r - q)
            wait_rows(None, beside, 0)
            pass_rows(has_above, beside, 0, r + q)
            pass_rows(has_below, beside, 0, r - q)
            if level == 0:
                load_c.wait()

                @pl.loop(0, slots)
                def _(k):
                    high, low = split(fac_f[k])
                    fac_w[k, :, 0:BS] = high
                    fac_w[k, :, BS : 2 * BS] = low

            for t in range(1, nc):
                from_below = group >= t
                from_above = group + t < nc
                for p, other in ((1, r), (0, r), (0, beside)):
                    low_r, high_r = other - q * t, other + q * t
                    wait_rows(from_below, low_r, p)
                    if t < nc - 1:
                        pass_rows(from_below & has_above, low_r, p, r + q)
                    if p:
                        pass_rows(from_below, low_r, p, beside)
                    wait_rows(from_above, high_r, p)
                    if t < nc - 1:
                        pass_rows(from_above & has_below, high_r, p, r - q)
                    if p:
                        pass_rows(from_above, high_r, p, beside)
                if level == 0 and t == 1:
                    make_selection(parent_s, row_v, col_v, sel, layout, hb, ns)
                    load_b.wait()

                    @pl.when(active)
                    def _():
                        split_inverse(inv_f, inv_h, inv_l, low_nodes, total)

            for z in range(nc):
                wait_rows(None, z * q + 1 - inner, 1)

    drain(pending)


def split_inverse(inv_f, inv_h, inv_l, begin, stop):
    chunk = 32
    rows = inv_f.shape[1]

    @pl.loop(begin, stop)
    def _(n):
        @pl.loop(0, rows // chunk)
        def _(i):
            part = pl.ds(pl.multiple_of(i * chunk, chunk), chunk)
            high, low = split(inv_f[n, part, :])
            inv_h[n, part, :] = high
            inv_l[n, part, :] = low


def make_selection(parent_s, row_v, col_v, sel, layout, hb, ns):
    row_block = row_v[...]
    row_node = row_block // NB
    walker = col_v[...] // NB
    valid = jnp.zeros(walker.shape, jnp.bool_)
    nodes = layout[-1][0] + 1
    for repeat in range(LEVELS - 1):
        moved = jnp.zeros_like(walker)
        for t in range(nodes):
            moved = jnp.where(walker == t, parent_s[t], moved)
        walker = moved
        valid = valid | (walker == row_node)
    inside = row_block % NB
    place = jnp.full(row_block.shape, -1, jnp.int32)
    low_nodes = layout[0][1]
    for begin, many in layout[1:]:
        spot = (
            (begin - low_nodes) * NB
            + (inside // hb) * (many * hb)
            + (row_node - begin) * hb
            + inside % hb
        )
        place = jnp.where(row_node >= begin, spot, place)
    place = jnp.where(valid, place, -1)
    count, slots = sel.shape
    rows = lax.broadcasted_iota(jnp.int32, (count, slots), 0)
    hits = rows == jnp.broadcast_to(place, (count, slots))
    sel[...] = jnp.where(hits, 1.0, 0.0).astype(jnp.bfloat16)


def fused_device(
    ns, nc, right_side, inverse_diag, factor_blocks, parent, node_order, block_row, block_col
):
    total, sc, rows_s = right_side.shape
    columns = inverse_diag.shape[2]
    slots = factor_blocks.shape[0]
    hb = rows_s // BS
    layout = level_layout()
    f32, bf16 = jnp.float32, jnp.bfloat16
    upper = total - layout[0][1]

    def per_level(lead, skip=0):
        return [pltpu.VMEM((*lead, m * hb, sc, BS), f32) for _, m in layout[skip:]]

    sems = pltpu.SemaphoreType.DMA
    scratch = [
        pltpu.VMEM((total, rows_s, columns), f32),
        pltpu.VMEM((total, rows_s, columns), bf16),
        pltpu.VMEM((total, rows_s, columns), bf16),
        pltpu.VMEM((slots, BS, BS), f32),
        pltpu.VMEM((slots, BS, 2 * BS), bf16),
        pltpu.VMEM((slots * sc, BS), f32),
        pltpu.VMEM((upper * NB, slots), bf16),
        pltpu.VMEM(((total - 1) * NB, sc, BS), f32),
        *per_level(()),
        *per_level((ns,)),
        *per_level((nc,)),
        *per_level((nc,)),
        *[pltpu.VMEM((m * NB, sc, BS), f32) for _, m in layout[1:]],
        *per_level((ns,), 1),
        sems((3,)),
        sems((LEVELS, ns)),
        sems((LEVELS, ns)),
        sems((LEVELS, 3, nc, 4)),
        sems((LEVELS, ns, 4)),
        sems((LEVELS, nc, 4)),
        sems((LEVELS, nc, 4)),
        sems((LEVELS - 1, 8 * nc)),
        sems((LEVELS - 1, 2, ns)),
    ]
    smem = pl.BlockSpec(memory_space=pltpu.SMEM)
    vmem = pl.BlockSpec(memory_space=pltpu.VMEM)
    hbm = pl.BlockSpec(memory_space=pl.ANY)
    return pl.pallas_call(
        functools.partial(kernel, ns, nc),
        out_shape=jax.ShapeDtypeStruct(right_side.shape, f32),
        in_specs=[smem, smem, smem, vmem, vmem, vmem, hbm, hbm],
        out_specs=vmem,
        scratch_shapes=scratch,
        compiler_params=pltpu.CompilerParams(
            collective_id=0, has_side_effects=True, vmem_limit_bytes=60 * 2**20
        ),
        name="substitute",
    )(
        parent,
        node_order,
        block_col,
        right_side,
        block_row[None, :],
        block_col[None, :],
        inverse_diag,
        factor_blocks,
    )


def solution(mesh):
    ns, nc = mesh.shape["sn"], mesh.shape["rhs"]
    in_specs = (
        P(None, "rhs", "sn"),
        P(None, "sn", "rhs"),
        P("sn", None, None),
        P(),
        P(),
        P("sn"),
        P("sn"),
    )
    out_specs = P(None, "rhs", "sn")
    fused = S % (ns * BS) == 0 and ns == 2 * nc and nc % 2 == 0
    body = functools.partial(fused_device, ns, nc) if fused else per_device
    return jax.shard_map(
        body, mesh=mesh, in_specs=in_specs, out_specs=out_specs, check_vma=False
    )
```

```python
import functools

import jax
import jax.numpy as jnp
from jax import lax
from jax.experimental import pallas as pl
from jax.experimental.pallas import tpu as pltpu
from jax.sharding import PartitionSpec as P

S = 2048
BS = 128
NB = 16
LEVELS = 4
PIECES = (4, 2, 2, 1)
CHAIN = (True, True, False, False)
TWO_STEP = (False, True, False, False)
BUFFERS = (
    ("own", 0),
    ("relay", 0),
    ("held", 0),
    ("stage", 0),
    ("terms", 0),
    ("part", 1),
    ("got", 1),
    ("cross", 1),
)


def level_layout():
    layout = []
    offset_value = 0
    for level_index in range(LEVELS):
        members = 2 ** (LEVELS - 1 - level_index)
        layout.append((offset_value, members))
        offset_value += members
    return layout


def to_blocks(values):
    count, scen_count, rows_total = values.shape
    return jnp.transpose(values.reshape(count, scen_count, NB, BS), (0, 2, 1, 3)).reshape(
        count * NB, scen_count, BS
    )


def from_blocks(values):
    count = values.shape[0] // NB
    scen_count = values.shape[1]
    return jnp.transpose(values.reshape(count, NB, scen_count, BS), (0, 2, 1, 3)).reshape(
        count, scen_count, NB * BS
    )


def table_lookup(table, index_values):
    hits = index_values[:, None] == jnp.arange(table.shape[0], dtype=jnp.int32)[None, :]
    return jnp.sum(jnp.where(hits, table[None, :], 0), axis=1)


def per_device(right_side, inverse_diag, factor_blocks, parent, node_order, block_row, block_col):
    node_total, sc_dev, rows_s = right_side.shape
    layout = level_layout()
    col_node = block_col // NB
    row_node = block_row // NB
    walker = col_node
    valid = jnp.zeros(col_node.shape, dtype=bool)
    for repeat in range(LEVELS - 1):
        walker = table_lookup(parent, walker)
        valid = valid | (walker == row_node)
    col_level = jnp.zeros(col_node.shape, jnp.int32)
    for level_index in range(1, LEVELS):
        col_level = col_level + (col_node >= layout[level_index][0]).astype(jnp.int32)
    own_offset = lax.axis_index("sn") * rows_s
    live = (jnp.arange(S, dtype=jnp.int32)[None, :] < node_order[:, None]).astype(jnp.float32)
    own_rows = own_offset + jnp.arange(rows_s, dtype=jnp.int32)
    live_own = (own_rows[None, :] < node_order[:, None]).astype(jnp.float32)
    partial_blocks = jnp.zeros((node_total * NB, sc_dev, BS), jnp.float32)
    solved_blocks = jnp.zeros((node_total * NB, sc_dev, BS), jnp.float32)
    pieces_out = []
    for level_index in range(LEVELS):
        first_node, members = layout[level_index]
        stop_node = first_node + members
        placed = lax.dynamic_update_slice_in_dim(
            jnp.zeros((members, sc_dev, S), jnp.float32),
            right_side[first_node:stop_node],
            own_offset,
            2,
        )
        r_term = placed - from_blocks(partial_blocks[first_node * NB : stop_node * NB])
        r_full = lax.psum(r_term, "sn")
        masked = r_full * live[first_node:stop_node, None, :]
        moved = lax.all_to_all(masked, "rhs", split_axis=2, concat_axis=1, tiled=True)
        block_inverse = inverse_diag[first_node:stop_node]

        def inverse_term(offset, length, moved=moved, block_inverse=block_inverse):
            return jnp.einsum("ncj,nij->cni", moved, block_inverse, precision=lax.Precision.HIGHEST)

        summed = lax.psum_scatter(
            inverse_term(jnp.int32(0), sc_dev * lax.axis_size("rhs")),
            "rhs",
            scatter_dimension=0,
            tiled=True,
        )
        y_piece = jnp.transpose(summed, (1, 0, 2))
        y_piece = y_piece * live_own[first_node:stop_node, None, :]
        pieces_out.append(y_piece)
        if level_index < LEVELS - 1:
            gathered = lax.all_gather(y_piece, "sn", axis=2, tiled=True)
            solved_blocks = solved_blocks.at[first_node * NB : stop_node * NB].set(
                to_blocks(gathered)
            )
            weights = (valid & (col_level == level_index)).astype(jnp.float32)
            columns = lax.map(
                lambda block, source=solved_blocks: lax.dynamic_index_in_dim(
                    source, block, 0, keepdims=False
                ),
                block_col,
            )
            update_terms = jnp.einsum(
                "kij,kcj->kci", factor_blocks, columns, precision=lax.Precision.HIGHEST
            )
            update_terms = update_terms * weights[:, None, None]
            partial_blocks = partial_blocks.at[block_row].add(update_terms)
    return jnp.concatenate(pieces_out, axis=0)


def split(values):
    high = values.astype(jnp.bfloat16)
    low = (values - high.astype(jnp.float32)).astype(jnp.bfloat16)
    return high, low


def dot_nt(left, right):
    return lax.dot_general(
        left, right, (((1,), (1,)), ((), ())), preferred_element_type=jnp.float32
    )


def kernel(
    ns,
    nc,
    parent_s,
    order_s,
    col_s,
    rhs_ref,
    row_v,
    col_v,
    inv_hbm,
    fac_hbm,
    out_hbm,
    *scratch,
):
    layout = level_layout()
    names = iter(scratch)
    inv_f, inv_h, inv_l, fac_f, fac_w, upd, sel, solved, out_v = [next(names) for _ in range(9)]
    buffers = {}
    for name, skip in BUFFERS:
        buffers[name] = [None] * skip + [next(names) for _ in layout[skip:]]
    load_sem, store_sem = next(names), next(names)
    x_send, x_recv, a_send, a_recv, b_send, b_recv, s_send, s_recv, c_send, c_recv, d_send, d_recv = [
        next(names) for _ in range(12)
    ]

    r = lax.axis_index("sn")
    c = lax.axis_index("rhs")
    nz, nx = nc, ns // nc
    z = r // nx
    x = r % nx
    active = c <= z
    above = z < nz - 1
    below = z > 0
    beside = r + 1 - 2 * x
    slots = fac_f.shape[0]
    sc = rhs_ref.shape[1]
    rows_s = rhs_ref.shape[2]
    hb = rows_s // BS
    low_nodes = layout[0][1]
    total = inv_f.shape[0]

    load_a = pltpu.make_async_copy(
        inv_hbm.at[pl.ds(0, low_nodes)], inv_f.at[pl.ds(0, low_nodes)], load_sem.at[0]
    )
    load_b = pltpu.make_async_copy(
        inv_hbm.at[pl.ds(low_nodes, total - low_nodes)],
        inv_f.at[pl.ds(low_nodes, total - low_nodes)],
        load_sem.at[1],
    )
    load_c = pltpu.make_async_copy(fac_hbm, fac_f, load_sem.at[2])
    load_a.start()
    load_c.start()
    load_b.start()

    barrier = pltpu.get_barrier_semaphore()
    partners = [(lax.rem(r + d, ns), c) for d in range(1, ns)]
    for dx in range(nx):
        for dc in range(1, nc):
            partners.append((z * nx + lax.rem(x + dx, nx), lax.rem(c + dc, nc)))
    for partner in partners:
        pl.semaphore_signal(
            barrier, inc=1, device_id=partner, device_id_type=pl.DeviceIdType.MESH
        )

    start_upper = low_nodes * NB

    @pl.loop(start_upper, solved.shape[0])
    def _(index):
        solved[index] = jnp.zeros((sc, BS), jnp.float32)

    def live_rows(node, h):
        lanes = lax.broadcasted_iota(jnp.int32, (sc, BS), 1) + (r * rows_s + h * BS)
        return lanes < order_s[node]

    def copy(src, dst, ssem, rsem, dev):
        return pltpu.make_async_remote_copy(
            src_ref=src,
            dst_ref=dst,
            send_sem=ssem,
            recv_sem=rsem,
            device_id=dev,
            device_id_type=pl.DeviceIdType.MESH,
        )

    def guard(cond, go):
        go() if cond is None else pl.when(cond)(go)

    def both_of(first_cond, second_cond):
        if first_cond is None:
            return second_cond
        return first_cond if second_cond is None else first_cond & second_cond

    def send(cond, src, dst, ssem, rsem, dev):
        guard(cond, lambda: copy(src, dst, ssem, rsem, dev).start())

    def arrived(cond, piece, sem):
        guard(cond, lambda: copy(piece, piece, sem, sem, (r, c)).wait_recv())

    waits = []

    def sent(cond, count, sem):
        def go():
            piece = solved.at[pl.ds(0, count)]
            copy(piece, piece, sem, sem, (r, c)).wait_send()

        waits.append((cond, go))

    def drain():
        for cond, go in waits:
            guard(cond, go)
        waits.clear()

    stores = []

    def run(level):
        first, members = layout[level]
        mh = members * hb
        base = first * NB
        pieces = PIECES[level]
        nodes = members // pieces
        size = nodes * hb
        own, relay, held, stage, terms, part, got, cross = [
            buffers[name][level]
            for name in ("own", "relay", "held", "stage", "terms", "part", "got", "cross")
        ]
        last = level == LEVELS - 1

        def rows(ch):
            return pl.ds(ch * size, size)

        def share(ch, to_z, to_x):
            return part.at[pl.ds(((ch * nx + to_x) * nz + to_z) * size, size)]

        def cross_send(ch):
            if TWO_STEP[level]:
                send(
                    None,
                    part.at[pl.ds((ch * nx + 1 - x) * nz * size, nz * size)],
                    cross.at[ch],
                    x_send.at[ch],
                    x_recv.at[ch],
                    (beside, c),
                )
                sent(None, nz * size, x_send.at[ch])
                return
            for d in range(1, ns):
                to = lax.rem(r + d, ns)
                send(
                    None,
                    share(ch, to // nx, to % nx),
                    got.at[ch, d - 1],
                    a_send.at[ch],
                    a_recv.at[ch],
                    (to, c),
                )
            sent(None, (ns - 1) * size, a_send.at[ch])

        def cross_sum(ch):
            if not TWO_STEP[level]:
                return
            arrived(None, cross.at[ch], x_recv.at[ch])

            @pl.loop(0, nz * size)
            def _(i):
                spot = (ch * nx + x) * nz * size + i
                part[spot] = part[spot] + cross[ch, i]

            for d in range(1, nz):
                to = lax.rem(z + d, nz)
                send(
                    None,
                    share(ch, to, x),
                    got.at[ch, d - 1],
                    a_send.at[ch],
                    a_recv.at[ch],
                    (to * nx + x, c),
                )
            sent(None, (nz - 1) * size, a_send.at[ch])

        def own_rows(ch):
            if level:
                arrived(None, got.at[ch], a_recv.at[ch])

            @pl.loop(0, nodes)
            def _(n):
                node = first + ch * nodes + n
                for h in range(hb):
                    i = n * hb + h
                    value = rhs_ref[node, :, h * BS : (h + 1) * BS]
                    if level:
                        value = value - part[((ch * nx + x) * nz + z) * size + i]
                        for d in range(got.shape[1]):
                            value = value - got[ch, d, i]
                    own[ch * size + i] = jnp.where(live_rows(node, h), value, 0.0)

        def spread(cond, zs, source, ch):
            slot = x * nc + c
            for way, to in enumerate((r, beside)):
                send(
                    both_of(cond, c != zs) if way == 0 else cond,
                    source.at[rows(ch)],
                    held.at[slot, rows(ch)],
                    s_send.at[ch],
                    s_recv.at[ch, slot],
                    (to, zs),
                )

            @pl.when(both_of(cond, c == zs))
            def _():
                @pl.loop(ch * size, (ch + 1) * size)
                def _(i):
                    held[slot, i] = source[i]

        def climb(cond, zs, source, ch, d):
            send(
                both_of(cond, z + d < nz),
                source.at[rows(ch)],
                relay.at[zs, rows(ch)],
                b_send.at[ch],
                b_recv.at[ch, zs],
                (r + nx * d, c),
            )

        def start_rows(ch):
            for d in range(1, 2 if CHAIN[level] else nz):
                climb(None, z, own, ch, d)
            spread(None, z, own, ch)
            for t in range(nz):
                climbs = (t + 1 if t < nz - 1 else 0) if CHAIN[level] else nz - 1 - t
                if climbs:
                    sent(z == t, climbs * size, b_send.at[ch])
                sent((z == t) & active, (2 * t + 1) * size, s_send.at[ch])
                if t < nz - 1:
                    sent((z == t) & (c > z), (2 * t + 2) * size, s_send.at[ch])

        def pass_rows(ch):
            for d in range(1, nz):
                zs = jnp.maximum(z - d, 0)
                arrived(z >= d, relay.at[zs, rows(ch)], b_recv.at[ch, zs])
                if CHAIN[level]:
                    climb(z >= d, zs, relay.at[zs], ch, 1)
                spread(z >= d, zs, relay.at[zs], ch)

        def product(ch):
            for dx in range(nx):
                for c2 in range(nc):
                    slot = lax.rem(x + dx, nx) * nc + c2
                    arrived(
                        both_of(active, c != c2) if dx == 0 else active,
                        held.at[slot, rows(ch)],
                        s_recv.at[ch, slot],
                    )

            @pl.when(active)
            def _():
                @pl.loop(ch * nodes, (ch + 1) * nodes)
                def _(n):
                    columns = []
                    for qi in range(nx):
                        for h in range(hb):
                            columns.append(
                                jnp.concatenate(
                                    [held[qi * nc + c2, n * hb + h] for c2 in range(nc)], axis=0
                                )
                            )
                    high, low = split(jnp.concatenate(columns, axis=1))
                    right_h = inv_h[first + n]
                    right_l = inv_l[first + n]
                    value = dot_nt(high, right_h) + (dot_nt(low, right_h) + dot_nt(high, right_l))
                    for c2 in range(nc):
                        for h in range(hb):
                            stage[c2, n * hb + h] = value[
                                c2 * sc : (c2 + 1) * sc, h * BS : (h + 1) * BS
                            ]
                    for h in range(hb):
                        terms[c, n * hb + h] = stage[c, n * hb + h]

            for d in range(1, nc):
                to = lax.rem(c + d, nc)
                send(
                    active,
                    stage.at[to, rows(ch)],
                    terms.at[c, rows(ch)],
                    c_send.at[ch],
                    c_recv.at[ch, c],
                    (r, to),
                )
            sent(active, (nc - 1) * size, c_send.at[ch])

        def rows_of(rs, ch):
            return solved.at[pl.ds(base + rs * mh + ch * size, size)]

        def gather(cond, rs, ch, to):
            send(
                cond, rows_of(rs, ch), rows_of(rs, ch), d_send.at[ch], d_recv.at[ch, rs], (to, c)
            )

        def collect(ch):
            for c2 in range(nc):
                arrived((c2 <= z) & (c != c2), terms.at[c2, rows(ch)], c_recv.at[ch, c2])
            for t in range(nz):

                @pl.when(z == t)
                def _(t=t):
                    @pl.loop(ch * nodes, (ch + 1) * nodes)
                    def _(n):
                        for h in range(hb):
                            i = n * hb + h
                            value = terms[0, i]
                            for c2 in range(1, t + 1):
                                value = value + terms[c2, i]
                            value = jnp.where(live_rows(first + n, h), value, 0.0)
                            out_v[first + n, :, h * BS : (h + 1) * BS] = value
                            if not last:
                                solved[base + r * mh + i] = value

            if last:
                return
            if CHAIN[level]:
                gather(above, r, ch, r + nx)
                gather(below, r, ch, r - nx)
            else:
                for d in range(1, nz):
                    gather(None, r, ch, lax.rem(z + d, nz) * nx + x)
            gather(None, r, ch, beside)

        def pass_solved(ch):
            if CHAIN[level]:
                for d in range(1, nz):
                    for step in (-1, 1):
                        there = z >= d if step < 0 else z + d < nz
                        rs = r + step * d * nx
                        arrived(there, rows_of(rs, ch), d_recv.at[ch, rs])
                        gather(there & (above if step < 0 else below), rs, ch, r - step * nx)
                        gather(there, rs, ch, beside)
                sent(above & below, (2 * nz + 1) * size, d_send.at[ch])
                sent((z == 0) | (z == nz - 1), (nz + 1) * size, d_send.at[ch])
                return
            for other in (z + 1 - 2 * (z % 2), lax.rem(z + 2, nz), nz - 1 - z):
                rs = other * nx + x
                arrived(None, rows_of(rs, ch), d_recv.at[ch, rs])
                gather(None, rs, ch, beside)
            sent(None, (2 * nz - 1) * size, d_send.at[ch])

        stages = [own_rows_and_start(own_rows, start_rows), pass_rows, product, collect]
        if level:
            for ch in range(pieces):
                cross_send(ch)
            stages.insert(0, cross_sum)
        else:
            for ch in range(pieces):
                own_rows(ch)
                if ch == 0:
                    pl.semaphore_wait(barrier, len(partners))
                start_rows(ch)
            stages.pop(0)
        if not last:
            stages.append(pass_solved)
        for t in range(pieces + len(stages) - 1):
            if level == 0 and t == 0:
                load_a.wait()

                @pl.when(active)
                def _():
                    split_inverse(inv_f, inv_h, inv_l, 0, low_nodes)

            if level == 0 and t == 1:
                make_selection(parent_s, row_v, col_v, sel, layout, hb, ns // nc, nc)
                load_c.wait()

                @pl.loop(0, slots)
                def _(k):
                    high, low = split(fac_f[k])
                    fac_w[k, :, 0:BS] = high
                    fac_w[k, :, BS : 2 * BS] = low

                load_b.wait()

                @pl.when(active)
                def _():
                    split_inverse(inv_f, inv_h, inv_l, low_nodes, total)

            for s, one in enumerate(stages):
                if 0 <= t - s < pieces:
                    one(t - s)
        store = pltpu.make_async_copy(
            out_v.at[pl.ds(first, members)],
            out_hbm.at[pl.ds(first, members)],
            store_sem.at[level],
        )
        store.start()
        stores.append(store)
        if not last:
            for ch in range(pieces):
                for other in range(nz):
                    rs = other * nx + 1 - x
                    arrived(None, rows_of(rs, ch), d_recv.at[ch, rs])

    def update(level):
        first, members = layout[level]
        part = buffers["part"][level]

        def one_block(k, carry):
            block = col_s[k]
            node = block // NB
            inside = block % NB
            offset = jnp.int32(0)
            count = jnp.int32(layout[0][1])
            for begin, many in layout[1:-1]:
                over = node >= begin
                offset = jnp.where(over, begin, offset)
                count = jnp.where(over, many, count)
            index = (
                offset * NB
                + (inside // hb) * (count * hb)
                + (node - offset) * hb
                + inside % hb
            )
            high, low = split(solved[index])
            left = jnp.concatenate(
                [
                    jnp.concatenate([high, high], axis=1),
                    jnp.concatenate([low, jnp.zeros_like(low)], axis=1),
                ],
                axis=0,
            )
            both = dot_nt(left, fac_w[k])
            upd[pl.ds(pl.multiple_of(k * sc, sc), sc), :] = both[:sc] + both[sc:]
            return carry

        lax.fori_loop(0, slots, one_block, 0, unroll=8)

        sel_first = (first - low_nodes) * NB
        picked = sel[sel_first : sel_first + members * NB, :]
        for s in range(0, sc, 2):
            pair = jnp.concatenate(
                [upd[pl.ds(s + t, slots, stride=sc), :] for t in range(2)], axis=1
            )
            high, low = split(pair)
            summed = jnp.dot(picked, high, preferred_element_type=jnp.float32) + jnp.dot(
                picked, low, preferred_element_type=jnp.float32
            )
            for t in range(2):
                part.reshape(members * NB * sc, BS)[
                    pl.ds(s + t, members * NB, stride=sc), :
                ] = summed[:, t * BS : (t + 1) * BS]

    for level in range(LEVELS):
        if level:
            update(level)
            drain()
        run(level)
    for store in stores:
        store.wait()
    drain()


def own_rows_and_start(own_rows, start_rows):
    def go(ch):
        own_rows(ch)
        start_rows(ch)

    return go


def split_inverse(inv_f, inv_h, inv_l, begin, stop):
    chunk = 32
    rows = inv_f.shape[1]

    @pl.loop(begin, stop)
    def _(n):
        @pl.loop(0, rows // chunk)
        def _(i):
            part = pl.ds(pl.multiple_of(i * chunk, chunk), chunk)
            high, low = split(inv_f[n, part, :])
            inv_h[n, part, :] = high
            inv_l[n, part, :] = low


def make_selection(parent_s, row_v, col_v, sel, layout, hb, nx, nz):
    row_block = row_v[...]
    row_node = row_block // NB
    walker = col_v[...] // NB
    valid = jnp.zeros(walker.shape, jnp.bool_)
    nodes = layout[-1][0] + 1
    for repeat in range(LEVELS - 1):
        moved = jnp.zeros_like(walker)
        for t in range(nodes):
            moved = jnp.where(walker == t, parent_s[t], moved)
        walker = moved
        valid = valid | (walker == row_node)
    inside = row_block % NB
    place = jnp.full(row_block.shape, -1, jnp.int32)
    low_nodes = layout[0][1]
    holder = inside // hb
    for level in range(1, LEVELS):
        begin, many = layout[level]
        nodes = many // PIECES[level]
        chunk = (row_node - begin) // nodes
        spot = (
            (begin - low_nodes) * NB
            + ((chunk * nx + holder % nx) * nz + holder // nx) * (nodes * hb)
            + (row_node - begin - chunk * nodes) * hb
            + inside % hb
        )
        place = jnp.where(row_node >= begin, spot, place)
    place = jnp.where(valid, place, -1)
    count, slots = sel.shape
    rows = lax.broadcasted_iota(jnp.int32, (count, slots), 0)
    hits = rows == jnp.broadcast_to(place, (count, slots))
    sel[...] = jnp.where(hits, 1.0, 0.0).astype(jnp.bfloat16)


def fused_device(
    ns, nc, right_side, inverse_diag, factor_blocks, parent, node_order, block_row, block_col
):
    total, sc, rows_s = right_side.shape
    columns = inverse_diag.shape[2]
    slots = factor_blocks.shape[0]
    hb = rows_s // BS
    layout = level_layout()
    f32, bf16 = jnp.float32, jnp.bfloat16
    upper = total - layout[0][1]


    def per_level(lead, skip=0):
        return [pltpu.VMEM((*lead, m * hb, sc, BS), f32) for _, m in layout[skip:]]

    def per_piece(lead):
        return [
            pltpu.VMEM((PIECES[k], *lead(k, layout[k][1] // PIECES[k] * hb), sc, BS), f32)
            for k in range(1, LEVELS)
        ]

    sems = pltpu.SemaphoreType.DMA
    most = max(PIECES)
    scratch = [
        pltpu.VMEM((total, rows_s, columns), f32),
        pltpu.VMEM((total, rows_s, columns), bf16),
        pltpu.VMEM((total, rows_s, columns), bf16),
        pltpu.VMEM((slots, BS, BS), f32),
        pltpu.VMEM((slots, BS, 2 * BS), bf16),
        pltpu.VMEM((slots * sc, BS), f32),
        pltpu.VMEM((upper * NB, slots), bf16),
        pltpu.VMEM(((total - 1) * NB, sc, BS), f32),
        pltpu.VMEM(right_side.shape, f32),
        *per_level(()),
        *per_level((nc - 1,)),
        *per_level((ns,)),
        *per_level((nc,)),
        *per_level((nc,)),
        *[pltpu.VMEM((m * NB, sc, BS), f32) for _, m in layout[1:]],
        *per_piece(lambda k, size: ((nc if TWO_STEP[k] else ns) - 1, size)),
        *per_piece(lambda k, size: ((nc if TWO_STEP[k] else 1) * size,)),
        sems((3,)),
        sems((LEVELS,)),
        sems((most,)),
        sems((most,)),
        sems((most,)),
        sems((most,)),
        sems((most,)),
        sems((most, nc - 1)),
        sems((most,)),
        sems((most, ns)),
        sems((most,)),
        sems((most, nc)),
        sems((most,)),
        sems((most, ns)),
    ]
    smem = pl.BlockSpec(memory_space=pltpu.SMEM)
    vmem = pl.BlockSpec(memory_space=pltpu.VMEM)
    hbm = pl.BlockSpec(memory_space=pl.ANY)
    return pl.pallas_call(
        functools.partial(kernel, ns, nc),
        out_shape=jax.ShapeDtypeStruct(right_side.shape, f32),
        in_specs=[smem, smem, smem, vmem, vmem, vmem, hbm, hbm],
        out_specs=hbm,
        scratch_shapes=scratch,
        compiler_params=pltpu.CompilerParams(
            collective_id=0, has_side_effects=True, vmem_limit_bytes=60 * 2**20
        ),
        name="substitute",
    )(
        parent,
        node_order,
        block_col,
        right_side,
        block_row[None, :],
        block_col[None, :],
        inverse_diag,
        factor_blocks,
    )


def solution(mesh):
    ns, nc = mesh.shape["sn"], mesh.shape["rhs"]
    in_specs = (
        P(None, "rhs", "sn"),
        P(None, "sn", "rhs"),
        P("sn", None, None),
        P(),
        P(),
        P("sn"),
        P("sn"),
    )
    out_specs = P(None, "rhs", "sn")
    fused = S % (ns * BS) == 0 and ns == 2 * nc and nc == 4
    body = functools.partial(fused_device, ns, nc) if fused else per_device
    return jax.shard_map(
        body, mesh=mesh, in_specs=in_specs, out_specs=out_specs, check_vma=False
    )
```

```python
import functools

import jax
import jax.numpy as jnp
from jax import lax
from jax.experimental import pallas as pl
from jax.experimental.pallas import tpu as pltpu
from jax.sharding import PartitionSpec as P

S = 2048
BS = 128
NB = 16
LEVELS = 4
PIECES = (4, 4, 2, 1)
CHAIN = ((False, True, True, True), (False, True, True, True), (False, False), (False,))
LAG = 1
CHAIN_BACK = ((True, True, True, True), (True, True, True, True), (False, False))
TWO_STEP = (False, True, False, False)
BUFFERS = (
    ("own", 0),
    ("relay", 0),
    ("held", 0),
    ("stage", 0),
    ("terms", 0),
    ("part", 1),
    ("got", 1),
    ("cross", 1),
)


def level_layout():
    layout = []
    offset_value = 0
    for level_index in range(LEVELS):
        members = 2 ** (LEVELS - 1 - level_index)
        layout.append((offset_value, members))
        offset_value += members
    return layout


def to_blocks(values):
    count, scen_count, rows_total = values.shape
    return jnp.transpose(values.reshape(count, scen_count, NB, BS), (0, 2, 1, 3)).reshape(
        count * NB, scen_count, BS
    )


def from_blocks(values):
    count = values.shape[0] // NB
    scen_count = values.shape[1]
    return jnp.transpose(values.reshape(count, NB, scen_count, BS), (0, 2, 1, 3)).reshape(
        count, scen_count, NB * BS
    )


def table_lookup(table, index_values):
    hits = index_values[:, None] == jnp.arange(table.shape[0], dtype=jnp.int32)[None, :]
    return jnp.sum(jnp.where(hits, table[None, :], 0), axis=1)


def per_device(right_side, inverse_diag, factor_blocks, parent, node_order, block_row, block_col):
    node_total, sc_dev, rows_s = right_side.shape
    layout = level_layout()
    col_node = block_col // NB
    row_node = block_row // NB
    walker = col_node
    valid = jnp.zeros(col_node.shape, dtype=bool)
    for repeat in range(LEVELS - 1):
        walker = table_lookup(parent, walker)
        valid = valid | (walker == row_node)
    col_level = jnp.zeros(col_node.shape, jnp.int32)
    for level_index in range(1, LEVELS):
        col_level = col_level + (col_node >= layout[level_index][0]).astype(jnp.int32)
    own_offset = lax.axis_index("sn") * rows_s
    live = (jnp.arange(S, dtype=jnp.int32)[None, :] < node_order[:, None]).astype(jnp.float32)
    own_rows = own_offset + jnp.arange(rows_s, dtype=jnp.int32)
    live_own = (own_rows[None, :] < node_order[:, None]).astype(jnp.float32)
    partial_blocks = jnp.zeros((node_total * NB, sc_dev, BS), jnp.float32)
    solved_blocks = jnp.zeros((node_total * NB, sc_dev, BS), jnp.float32)
    pieces_out = []
    for level_index in range(LEVELS):
        first_node, members = layout[level_index]
        stop_node = first_node + members
        placed = lax.dynamic_update_slice_in_dim(
            jnp.zeros((members, sc_dev, S), jnp.float32),
            right_side[first_node:stop_node],
            own_offset,
            2,
        )
        r_term = placed - from_blocks(partial_blocks[first_node * NB : stop_node * NB])
        r_full = lax.psum(r_term, "sn")
        masked = r_full * live[first_node:stop_node, None, :]
        moved = lax.all_to_all(masked, "rhs", split_axis=2, concat_axis=1, tiled=True)
        block_inverse = inverse_diag[first_node:stop_node]

        def inverse_term(offset, length, moved=moved, block_inverse=block_inverse):
            return jnp.einsum("ncj,nij->cni", moved, block_inverse, precision=lax.Precision.HIGHEST)

        summed = lax.psum_scatter(
            inverse_term(jnp.int32(0), sc_dev * lax.axis_size("rhs")),
            "rhs",
            scatter_dimension=0,
            tiled=True,
        )
        y_piece = jnp.transpose(summed, (1, 0, 2))
        y_piece = y_piece * live_own[first_node:stop_node, None, :]
        pieces_out.append(y_piece)
        if level_index < LEVELS - 1:
            gathered = lax.all_gather(y_piece, "sn", axis=2, tiled=True)
            solved_blocks = solved_blocks.at[first_node * NB : stop_node * NB].set(
                to_blocks(gathered)
            )
            weights = (valid & (col_level == level_index)).astype(jnp.float32)
            columns = lax.map(
                lambda block, source=solved_blocks: lax.dynamic_index_in_dim(
                    source, block, 0, keepdims=False
                ),
                block_col,
            )
            update_terms = jnp.einsum(
                "kij,kcj->kci", factor_blocks, columns, precision=lax.Precision.HIGHEST
            )
            update_terms = update_terms * weights[:, None, None]
            partial_blocks = partial_blocks.at[block_row].add(update_terms)
    return jnp.concatenate(pieces_out, axis=0)


def split(values):
    high = values.astype(jnp.bfloat16)
    low = (values - high.astype(jnp.float32)).astype(jnp.bfloat16)
    return high, low


def dot_nt(left, right):
    return lax.dot_general(
        left, right, (((1,), (1,)), ((), ())), preferred_element_type=jnp.float32
    )


def kernel(
    ns,
    nc,
    parent_s,
    order_s,
    col_s,
    rhs_ref,
    row_v,
    col_v,
    inv_hbm,
    fac_hbm,
    out_hbm,
    *scratch,
):
    layout = level_layout()
    names = iter(scratch)
    inv_f, inv_h, inv_l, fac_f, fac_w, upd, sel, solved, out_v = [next(names) for _ in range(9)]
    buffers = {}
    for name, skip in BUFFERS:
        buffers[name] = [None] * skip + [next(names) for _ in layout[skip:]]
    load_sem, store_sem = next(names), next(names)
    x_send, x_recv, a_send, a_recv, b_send, b_recv, s_send, s_recv, c_send, c_recv, d_send, d_recv = [
        next(names) for _ in range(12)
    ]

    r = lax.axis_index("sn")
    c = lax.axis_index("rhs")
    nz, nx = nc, ns // nc
    z = r // nx
    x = r % nx
    active = c <= z
    above = z < nz - 1
    below = z > 0
    beside = r + 1 - 2 * x
    slots = fac_f.shape[0]
    sc = rhs_ref.shape[1]
    rows_s = rhs_ref.shape[2]
    hb = rows_s // BS
    low_nodes = layout[0][1]
    total = inv_f.shape[0]

    load_a = pltpu.make_async_copy(
        inv_hbm.at[pl.ds(0, low_nodes)], inv_f.at[pl.ds(0, low_nodes)], load_sem.at[0]
    )
    load_b = pltpu.make_async_copy(
        inv_hbm.at[pl.ds(low_nodes, total - low_nodes)],
        inv_f.at[pl.ds(low_nodes, total - low_nodes)],
        load_sem.at[1],
    )
    load_c = pltpu.make_async_copy(fac_hbm, fac_f, load_sem.at[2])
    load_a.start()
    load_c.start()
    load_b.start()

    barrier = pltpu.get_barrier_semaphore()
    partners = [(lax.rem(r + d, ns), c) for d in range(1, ns)]
    for dx in range(nx):
        for dc in range(1, nc):
            partners.append((z * nx + lax.rem(x + dx, nx), lax.rem(c + dc, nc)))
    for partner in partners:
        pl.semaphore_signal(
            barrier, inc=1, device_id=partner, device_id_type=pl.DeviceIdType.MESH
        )

    start_upper = low_nodes * NB

    @pl.loop(start_upper, solved.shape[0])
    def _(index):
        solved[index] = jnp.zeros((sc, BS), jnp.float32)

    def live_rows(node, h):
        lanes = lax.broadcasted_iota(jnp.int32, (sc, BS), 1) + (r * rows_s + h * BS)
        return lanes < order_s[node]

    def copy(src, dst, ssem, rsem, dev):
        return pltpu.make_async_remote_copy(
            src_ref=src,
            dst_ref=dst,
            send_sem=ssem,
            recv_sem=rsem,
            device_id=dev,
            device_id_type=pl.DeviceIdType.MESH,
        )

    def guard(cond, go):
        go() if cond is None else pl.when(cond)(go)

    def both_of(first_cond, second_cond):
        if first_cond is None:
            return second_cond
        return first_cond if second_cond is None else first_cond & second_cond

    def send(cond, src, dst, ssem, rsem, dev):
        guard(cond, lambda: copy(src, dst, ssem, rsem, dev).start())

    def arrived(cond, piece, sem):
        guard(cond, lambda: copy(piece, piece, sem, sem, (r, c)).wait_recv())

    waits = []

    def sent(cond, count, sem):
        def go():
            piece = solved.at[pl.ds(0, count)]
            copy(piece, piece, sem, sem, (r, c)).wait_send()

        waits.append((cond, go))

    def drain():
        for cond, go in waits:
            guard(cond, go)
        waits.clear()

    stores = []

    def run(level):
        first, members = layout[level]
        mh = members * hb
        base = first * NB
        pieces = PIECES[level]
        nodes = members // pieces
        size = nodes * hb
        own, relay, held, stage, terms, part, got, cross = [
            buffers[name][level]
            for name in ("own", "relay", "held", "stage", "terms", "part", "got", "cross")
        ]
        last = level == LEVELS - 1

        def rows(ch):
            return pl.ds(ch * size, size)

        def share(ch, to_z, to_x):
            return part.at[pl.ds(((ch * nx + to_x) * nz + to_z) * size, size)]

        def cross_send(ch):
            if TWO_STEP[level]:
                send(
                    None,
                    part.at[pl.ds((ch * nx + 1 - x) * nz * size, nz * size)],
                    cross.at[ch],
                    x_send.at[ch],
                    x_recv.at[ch],
                    (beside, c),
                )
                sent(None, nz * size, x_send.at[ch])
                return
            for d in range(1, ns):
                to = lax.rem(r + d, ns)
                send(
                    None,
                    share(ch, to // nx, to % nx),
                    got.at[ch, d - 1],
                    a_send.at[ch],
                    a_recv.at[ch],
                    (to, c),
                )
            sent(None, (ns - 1) * size, a_send.at[ch])

        def cross_sum(ch):
            if not TWO_STEP[level]:
                return
            arrived(None, cross.at[ch], x_recv.at[ch])

            @pl.loop(0, nz * size)
            def _(i):
                spot = (ch * nx + x) * nz * size + i
                part[spot] = part[spot] + cross[ch, i]

            for d in range(1, nz):
                to = lax.rem(z + d, nz)
                send(
                    None,
                    share(ch, to, x),
                    got.at[ch, d - 1],
                    a_send.at[ch],
                    a_recv.at[ch],
                    (to * nx + x, c),
                )
            sent(None, (nz - 1) * size, a_send.at[ch])

        def own_rows(ch):
            if level:
                arrived(None, got.at[ch], a_recv.at[ch])

            @pl.loop(0, nodes)
            def _(n):
                node = first + ch * nodes + n
                for h in range(hb):
                    i = n * hb + h
                    value = rhs_ref[node, :, h * BS : (h + 1) * BS]
                    if level:
                        value = value - part[((ch * nx + x) * nz + z) * size + i]
                        for d in range(got.shape[1]):
                            value = value - got[ch, d, i]
                    own[ch * size + i] = jnp.where(live_rows(node, h), value, 0.0)

        def spread(cond, zs, source, ch):
            slot = x * nc + c
            for way, to in enumerate((r, beside)):
                send(
                    both_of(cond, c != zs) if way == 0 else cond,
                    source.at[rows(ch)],
                    held.at[slot, rows(ch)],
                    s_send.at[ch],
                    s_recv.at[ch, slot],
                    (to, zs),
                )

            @pl.when(both_of(cond, c == zs))
            def _():
                @pl.loop(ch * size, (ch + 1) * size)
                def _(i):
                    held[slot, i] = source[i]

        def climb(cond, zs, source, ch, d):
            send(
                both_of(cond, z + d < nz),
                source.at[rows(ch)],
                relay.at[zs, rows(ch)],
                b_send.at[ch],
                b_recv.at[ch, zs],
                (r + nx * d, c),
            )

        def start_rows(ch):
            for d in range(1, 2 if CHAIN[level][ch] else nz):
                climb(None, z, own, ch, d)
            if level:
                spread(None, z, own, ch)
            for t in range(nz):
                climbs = (t + 1 if t < nz - 1 else 0) if CHAIN[level][ch] else nz - 1 - t
                if climbs:
                    sent(z == t, climbs * size, b_send.at[ch])
                sent((z == t) & active, (2 * t + 1) * size, s_send.at[ch])
                if t < nz - 1:
                    sent((z == t) & (c > z), (2 * t + 2) * size, s_send.at[ch])

        def pass_rows(ch):
            for d in range(1, nz):
                zs = jnp.maximum(z - d, 0)
                arrived(z >= d, relay.at[zs, rows(ch)], b_recv.at[ch, zs])
                if CHAIN[level][ch]:
                    climb(z >= d, zs, relay.at[zs], ch, 1)
                spread(z >= d, zs, relay.at[zs], ch)
            if level == 0:
                spread(None, z, own, ch)

        def product(ch):
            for dx in range(nx):
                for c2 in range(nc):
                    slot = lax.rem(x + dx, nx) * nc + c2
                    arrived(
                        both_of(active, c != c2) if dx == 0 else active,
                        held.at[slot, rows(ch)],
                        s_recv.at[ch, slot],
                    )

            @pl.when(active)
            def _():
                @pl.loop(ch * nodes, (ch + 1) * nodes)
                def _(n):
                    columns = []
                    for qi in range(nx):
                        for h in range(hb):
                            columns.append(
                                jnp.concatenate(
                                    [held[qi * nc + c2, n * hb + h] for c2 in range(nc)], axis=0
                                )
                            )
                    high, low = split(jnp.concatenate(columns, axis=1))
                    right_h = inv_h[first + n]
                    right_l = inv_l[first + n]
                    value = dot_nt(high, right_h) + (dot_nt(low, right_h) + dot_nt(high, right_l))
                    for c2 in range(nc):
                        for h in range(hb):
                            stage[c2, n * hb + h] = value[
                                c2 * sc : (c2 + 1) * sc, h * BS : (h + 1) * BS
                            ]
                    for h in range(hb):
                        terms[c, n * hb + h] = stage[c, n * hb + h]

            for d in range(1, nc):
                to = lax.rem(c + d, nc)
                send(
                    active,
                    stage.at[to, rows(ch)],
                    terms.at[c, rows(ch)],
                    c_send.at[ch],
                    c_recv.at[ch, c],
                    (r, to),
                )
            sent(active, (nc - 1) * size, c_send.at[ch])

        def rows_of(rs, ch):
            return solved.at[pl.ds(base + rs * mh + ch * size, size)]

        def gather(cond, rs, ch, to):
            send(
                cond, rows_of(rs, ch), rows_of(rs, ch), d_send.at[ch], d_recv.at[ch, rs], (to, c)
            )

        def collect(ch):
            for c2 in range(nc):
                arrived((c2 <= z) & (c != c2), terms.at[c2, rows(ch)], c_recv.at[ch, c2])
            for t in range(nz):

                @pl.when(z == t)
                def _(t=t):
                    @pl.loop(ch * nodes, (ch + 1) * nodes)
                    def _(n):
                        for h in range(hb):
                            i = n * hb + h
                            value = terms[0, i]
                            for c2 in range(1, t + 1):
                                value = value + terms[c2, i]
                            value = jnp.where(live_rows(first + n, h), value, 0.0)
                            out_v[first + n, :, h * BS : (h + 1) * BS] = value
                            if not last:
                                solved[base + r * mh + i] = value

            if last:
                return
            if CHAIN_BACK[level][ch]:
                gather(above, r, ch, r + nx)
                gather(below, r, ch, r - nx)
            else:
                for d in range(1, nz):
                    gather(None, r, ch, lax.rem(z + d, nz) * nx + x)
            gather(None, r, ch, beside)

        def pass_one(ch, step, d, cond=None):
            there = both_of(cond, z >= d if step < 0 else z + d < nz)
            rs = r + step * d * nx
            arrived(there, rows_of(rs, ch), d_recv.at[ch, rs])
            if CHAIN_BACK[level][ch]:
                gather(there & (above if step < 0 else below), rs, ch, r - step * nx)
            gather(there, rs, ch, beside)

        def pass_lower(ch):
            for d in range(1, nz):
                pass_one(ch, -1, d)

        early = range(2 if pieces > 2 else 0)

        def pass_early(ch):
            if ch in early:
                pass_one(ch, 1, 1, z == nz - 2)

        def pass_upper():
            order = [(2 * ch + LAG * (d - 1), d, ch) for ch in range(pieces) for d in range(1, nz)]
            for _, d, ch in sorted(order):
                pass_one(ch, 1, d, z < nz - 2 if d == 1 and ch in early else None)
            for ch in range(pieces):
                if CHAIN_BACK[level][ch]:
                    sent(above & below, (2 * nz + 1) * size, d_send.at[ch])
                    sent((z == 0) | (z == nz - 1), (nz + 1) * size, d_send.at[ch])
                else:
                    sent(None, (2 * nz - 1) * size, d_send.at[ch])

        stages = [own_rows_and_start(own_rows, start_rows), pass_rows, product, collect]
        if level:
            for ch in range(pieces):
                cross_send(ch)
            stages.insert(0, cross_sum)
        else:
            for ch in range(pieces):
                own_rows(ch)
                if ch == 0:
                    pl.semaphore_wait(barrier, len(partners))
                start_rows(ch)
            stages.pop(0)
        if not last:
            stages.append(pass_lower)
        for t in range(pieces + len(stages) - 1):
            if level == 0 and t == 0:
                load_a.wait()

                @pl.when(active)
                def _():
                    split_inverse(inv_f, inv_h, inv_l, 0, low_nodes)

            if level == 0 and t == 1:
                make_selection(parent_s, row_v, col_v, sel, layout, hb, ns // nc, nc)
                load_c.wait()

                @pl.loop(0, slots)
                def _(k):
                    high, low = split(fac_f[k])
                    fac_w[k, :, 0:BS] = high
                    fac_w[k, :, BS : 2 * BS] = low

                load_b.wait()

                @pl.when(active)
                def _():
                    split_inverse(inv_f, inv_h, inv_l, low_nodes, total)

            passed = t - stages.index(collect)
            if passed == 2:
                pass_early(0)
            for s, one in enumerate(stages):
                if 0 <= t - s < pieces:
                    one(t - s)
            if passed == 3:
                pass_early(1)
        if not last:
            pass_upper()
        store = pltpu.make_async_copy(
            out_v.at[pl.ds(first, members)],
            out_hbm.at[pl.ds(first, members)],
            store_sem.at[level],
        )
        store.start()
        stores.append(store)
        if not last:
            for ch in range(pieces):
                for other in range(nz):
                    rs = other * nx + 1 - x
                    arrived(None, rows_of(rs, ch), d_recv.at[ch, rs])

    def update(level):
        first, members = layout[level]
        part = buffers["part"][level]

        def one_block(k, carry):
            block = col_s[k]
            node = block // NB
            inside = block % NB
            offset = jnp.int32(0)
            count = jnp.int32(layout[0][1])
            for begin, many in layout[1:-1]:
                over = node >= begin
                offset = jnp.where(over, begin, offset)
                count = jnp.where(over, many, count)
            index = (
                offset * NB
                + (inside // hb) * (count * hb)
                + (node - offset) * hb
                + inside % hb
            )
            high, low = split(solved[index])
            left = jnp.concatenate(
                [
                    jnp.concatenate([high, high], axis=1),
                    jnp.concatenate([low, jnp.zeros_like(low)], axis=1),
                ],
                axis=0,
            )
            both = dot_nt(left, fac_w[k])
            upd[pl.ds(pl.multiple_of(k * sc, sc), sc), :] = both[:sc] + both[sc:]
            return carry

        lax.fori_loop(0, slots, one_block, 0, unroll=slots // 2)

        sel_first = (first - low_nodes) * NB
        picked = sel[sel_first : sel_first + members * NB, :]
        for s in range(0, sc, 2):
            pair = jnp.concatenate(
                [upd[pl.ds(s + t, slots, stride=sc), :] for t in range(2)], axis=1
            )
            summed = jnp.dot(
                picked,
                jnp.concatenate(split(pair), axis=0),
                preferred_element_type=jnp.float32,
            )
            for t in range(2):
                part.reshape(members * NB * sc, BS)[
                    pl.ds(s + t, members * NB, stride=sc), :
                ] = summed[:, t * BS : (t + 1) * BS]

    for level in range(LEVELS):
        if level:
            update(level)
            drain()
        run(level)
    for store in stores:
        store.wait()
    drain()


def own_rows_and_start(own_rows, start_rows):
    def go(ch):
        own_rows(ch)
        start_rows(ch)

    return go


def split_inverse(inv_f, inv_h, inv_l, begin, stop):
    chunk = 32
    rows = inv_f.shape[1]

    @pl.loop(begin, stop)
    def _(n):
        @pl.loop(0, rows // chunk)
        def _(i):
            part = pl.ds(pl.multiple_of(i * chunk, chunk), chunk)
            high, low = split(inv_f[n, part, :])
            inv_h[n, part, :] = high
            inv_l[n, part, :] = low


def make_selection(parent_s, row_v, col_v, sel, layout, hb, nx, nz):
    row_block = row_v[...]
    row_node = row_block // NB
    walker = col_v[...] // NB
    valid = jnp.zeros(walker.shape, jnp.bool_)
    nodes = layout[-1][0] + 1
    for repeat in range(LEVELS - 1):
        moved = jnp.zeros_like(walker)
        for t in range(nodes):
            moved = jnp.where(walker == t, parent_s[t], moved)
        walker = moved
        valid = valid | (walker == row_node)
    inside = row_block % NB
    place = jnp.full(row_block.shape, -1, jnp.int32)
    low_nodes = layout[0][1]
    holder = inside // hb
    for level in range(1, LEVELS):
        begin, many = layout[level]
        nodes = many // PIECES[level]
        chunk = (row_node - begin) // nodes
        spot = (
            (begin - low_nodes) * NB
            + ((chunk * nx + holder % nx) * nz + holder // nx) * (nodes * hb)
            + (row_node - begin - chunk * nodes) * hb
            + inside % hb
        )
        place = jnp.where(row_node >= begin, spot, place)
    place = jnp.where(valid, place, -1)
    count, slots = sel.shape[0], row_block.shape[1]
    rows = lax.broadcasted_iota(jnp.int32, (count, slots), 0)
    hits = rows == jnp.broadcast_to(place, (count, slots))
    once = jnp.where(hits, 1.0, 0.0).astype(jnp.bfloat16)
    sel[...] = jnp.concatenate([once, once], axis=1)


def fused_device(
    ns, nc, right_side, inverse_diag, factor_blocks, parent, node_order, block_row, block_col
):
    total, sc, rows_s = right_side.shape
    columns = inverse_diag.shape[2]
    slots = factor_blocks.shape[0]
    hb = rows_s // BS
    layout = level_layout()
    f32, bf16 = jnp.float32, jnp.bfloat16
    upper = total - layout[0][1]


    def per_level(lead, skip=0):
        return [pltpu.VMEM((*lead, m * hb, sc, BS), f32) for _, m in layout[skip:]]

    def per_piece(lead):
        return [
            pltpu.VMEM((PIECES[k], *lead(k, layout[k][1] // PIECES[k] * hb), sc, BS), f32)
            for k in range(1, LEVELS)
        ]

    sems = pltpu.SemaphoreType.DMA
    most = max(PIECES)
    scratch = [
        pltpu.VMEM((total, rows_s, columns), f32),
        pltpu.VMEM((total, rows_s, columns), bf16),
        pltpu.VMEM((total, rows_s, columns), bf16),
        pltpu.VMEM((slots, BS, BS), f32),
        pltpu.VMEM((slots, BS, 2 * BS), bf16),
        pltpu.VMEM((slots * sc, BS), f32),
        pltpu.VMEM((upper * NB, 2 * slots), bf16),
        pltpu.VMEM(((total - 1) * NB, sc, BS), f32),
        pltpu.VMEM(right_side.shape, f32),
        *per_level(()),
        *per_level((nc - 1,)),
        *per_level((ns,)),
        *per_level((nc,)),
        *per_level((nc,)),
        *[pltpu.VMEM((m * NB, sc, BS), f32) for _, m in layout[1:]],
        *per_piece(lambda k, size: ((nc if TWO_STEP[k] else ns) - 1, size)),
        *per_piece(lambda k, size: ((nc if TWO_STEP[k] else 1) * size,)),
        sems((3,)),
        sems((LEVELS,)),
        sems((most,)),
        sems((most,)),
        sems((most,)),
        sems((most,)),
        sems((most,)),
        sems((most, nc - 1)),
        sems((most,)),
        sems((most, ns)),
        sems((most,)),
        sems((most, nc)),
        sems((most,)),
        sems((most, ns)),
    ]
    smem = pl.BlockSpec(memory_space=pltpu.SMEM)
    vmem = pl.BlockSpec(memory_space=pltpu.VMEM)
    hbm = pl.BlockSpec(memory_space=pl.ANY)
    return pl.pallas_call(
        functools.partial(kernel, ns, nc),
        out_shape=jax.ShapeDtypeStruct(right_side.shape, f32),
        in_specs=[smem, smem, smem, vmem, vmem, vmem, hbm, hbm],
        out_specs=hbm,
        scratch_shapes=scratch,
        compiler_params=pltpu.CompilerParams(
            collective_id=0, has_side_effects=True, vmem_limit_bytes=60 * 2**20
        ),
        name="substitute",
    )(
        parent,
        node_order,
        block_col,
        right_side,
        block_row[None, :],
        block_col[None, :],
        inverse_diag,
        factor_blocks,
    )


def solution(mesh):
    ns, nc = mesh.shape["sn"], mesh.shape["rhs"]
    in_specs = (
        P(None, "rhs", "sn"),
        P(None, "sn", "rhs"),
        P("sn", None, None),
        P(),
        P(),
        P("sn"),
        P("sn"),
    )
    out_specs = P(None, "rhs", "sn")
    fused = S % (ns * BS) == 0 and ns == 2 * nc and nc == 4
    body = functools.partial(fused_device, ns, nc) if fused else per_device
    return jax.shard_map(
        body, mesh=mesh, in_specs=in_specs, out_specs=out_specs, check_vma=False
    )
```

```python
import functools

import jax
import jax.numpy as jnp
from jax import lax
from jax.experimental import pallas as pl
from jax.experimental.pallas import tpu as pltpu
from jax.sharding import PartitionSpec as P

S = 2048
BS = 128
NB = 16
LEVELS = 4
PIECES = (4, 4, 2, 1)
CHAIN = ((False, True, True, True), (False, True, True, True), (False, False), (False,))
LAG = 1
CHAIN_BACK = ((True, True, True, True), (True, True, True, True), (False, False))
TWO_STEP = (None, (True, True, True, False), (True, False), (False,))
BUFFERS = (
    ("own", 0),
    ("relay", 0),
    ("held", 0),
    ("stage", 0),
    ("terms", 0),
    ("part", 1),
    ("got", 1),
    ("cross", 1),
)


def level_layout():
    layout = []
    offset_value = 0
    for level_index in range(LEVELS):
        members = 2 ** (LEVELS - 1 - level_index)
        layout.append((offset_value, members))
        offset_value += members
    return layout


def to_blocks(values):
    count, scen_count, rows_total = values.shape
    return jnp.transpose(values.reshape(count, scen_count, NB, BS), (0, 2, 1, 3)).reshape(
        count * NB, scen_count, BS
    )


def from_blocks(values):
    count = values.shape[0] // NB
    scen_count = values.shape[1]
    return jnp.transpose(values.reshape(count, NB, scen_count, BS), (0, 2, 1, 3)).reshape(
        count, scen_count, NB * BS
    )


def table_lookup(table, index_values):
    hits = index_values[:, None] == jnp.arange(table.shape[0], dtype=jnp.int32)[None, :]
    return jnp.sum(jnp.where(hits, table[None, :], 0), axis=1)


def per_device(right_side, inverse_diag, factor_blocks, parent, node_order, block_row, block_col):
    node_total, sc_dev, rows_s = right_side.shape
    layout = level_layout()
    col_node = block_col // NB
    row_node = block_row // NB
    walker = col_node
    valid = jnp.zeros(col_node.shape, dtype=bool)
    for repeat in range(LEVELS - 1):
        walker = table_lookup(parent, walker)
        valid = valid | (walker == row_node)
    col_level = jnp.zeros(col_node.shape, jnp.int32)
    for level_index in range(1, LEVELS):
        col_level = col_level + (col_node >= layout[level_index][0]).astype(jnp.int32)
    own_offset = lax.axis_index("sn") * rows_s
    live = (jnp.arange(S, dtype=jnp.int32)[None, :] < node_order[:, None]).astype(jnp.float32)
    own_rows = own_offset + jnp.arange(rows_s, dtype=jnp.int32)
    live_own = (own_rows[None, :] < node_order[:, None]).astype(jnp.float32)
    partial_blocks = jnp.zeros((node_total * NB, sc_dev, BS), jnp.float32)
    solved_blocks = jnp.zeros((node_total * NB, sc_dev, BS), jnp.float32)
    pieces_out = []
    for level_index in range(LEVELS):
        first_node, members = layout[level_index]
        stop_node = first_node + members
        placed = lax.dynamic_update_slice_in_dim(
            jnp.zeros((members, sc_dev, S), jnp.float32),
            right_side[first_node:stop_node],
            own_offset,
            2,
        )
        r_term = placed - from_blocks(partial_blocks[first_node * NB : stop_node * NB])
        r_full = lax.psum(r_term, "sn")
        masked = r_full * live[first_node:stop_node, None, :]
        moved = lax.all_to_all(masked, "rhs", split_axis=2, concat_axis=1, tiled=True)
        block_inverse = inverse_diag[first_node:stop_node]

        def inverse_term(offset, length, moved=moved, block_inverse=block_inverse):
            return jnp.einsum("ncj,nij->cni", moved, block_inverse, precision=lax.Precision.HIGHEST)

        summed = lax.psum_scatter(
            inverse_term(jnp.int32(0), sc_dev * lax.axis_size("rhs")),
            "rhs",
            scatter_dimension=0,
            tiled=True,
        )
        y_piece = jnp.transpose(summed, (1, 0, 2))
        y_piece = y_piece * live_own[first_node:stop_node, None, :]
        pieces_out.append(y_piece)
        if level_index < LEVELS - 1:
            gathered = lax.all_gather(y_piece, "sn", axis=2, tiled=True)
            solved_blocks = solved_blocks.at[first_node * NB : stop_node * NB].set(
                to_blocks(gathered)
            )
            weights = (valid & (col_level == level_index)).astype(jnp.float32)
            columns = lax.map(
                lambda block, source=solved_blocks: lax.dynamic_index_in_dim(
                    source, block, 0, keepdims=False
                ),
                block_col,
            )
            update_terms = jnp.einsum(
                "kij,kcj->kci", factor_blocks, columns, precision=lax.Precision.HIGHEST
            )
            update_terms = update_terms * weights[:, None, None]
            partial_blocks = partial_blocks.at[block_row].add(update_terms)
    return jnp.concatenate(pieces_out, axis=0)


def split(values):
    high = values.astype(jnp.bfloat16)
    low = (values - high.astype(jnp.float32)).astype(jnp.bfloat16)
    return high, low


def dot_nt(left, right):
    return lax.dot_general(
        left, right, (((1,), (1,)), ((), ())), preferred_element_type=jnp.float32
    )


def kernel(
    ns,
    nc,
    parent_s,
    order_s,
    col_s,
    rhs_ref,
    row_v,
    col_v,
    inv_hbm,
    fac_hbm,
    out_hbm,
    *scratch,
):
    layout = level_layout()
    names = iter(scratch)
    inv_f, inv_h, inv_l, fac_f, fac_w, upd, sel, solved, out_v = [next(names) for _ in range(9)]
    buffers = {}
    for name, skip in BUFFERS:
        buffers[name] = [None] * skip + [next(names) for _ in layout[skip:]]
    load_sem, store_sem = next(names), next(names)
    x_send, x_recv, a_send, a_recv, b_send, b_recv, s_send, s_recv, c_send, c_recv, d_send, d_recv = [
        next(names) for _ in range(12)
    ]

    r = lax.axis_index("sn")
    c = lax.axis_index("rhs")
    nz, nx = nc, ns // nc
    z = r // nx
    x = r % nx
    active = c <= z
    above = z < nz - 1
    below = z > 0
    beside = r + 1 - 2 * x
    slots = fac_f.shape[0]
    sc = rhs_ref.shape[1]
    rows_s = rhs_ref.shape[2]
    hb = rows_s // BS
    low_nodes = layout[0][1]
    total = inv_f.shape[0]

    load_a = pltpu.make_async_copy(
        inv_hbm.at[pl.ds(0, low_nodes)], inv_f.at[pl.ds(0, low_nodes)], load_sem.at[0]
    )
    load_b = pltpu.make_async_copy(
        inv_hbm.at[pl.ds(low_nodes, total - low_nodes)],
        inv_f.at[pl.ds(low_nodes, total - low_nodes)],
        load_sem.at[1],
    )
    load_c = pltpu.make_async_copy(fac_hbm, fac_f, load_sem.at[2])
    load_a.start()
    load_c.start()
    load_b.start()

    barrier = pltpu.get_barrier_semaphore()
    partners = [(lax.rem(r + d, ns), c) for d in range(1, ns)]
    for dx in range(nx):
        for dc in range(1, nc):
            partners.append((z * nx + lax.rem(x + dx, nx), lax.rem(c + dc, nc)))
    for partner in partners:
        pl.semaphore_signal(
            barrier, inc=1, device_id=partner, device_id_type=pl.DeviceIdType.MESH
        )

    start_upper = low_nodes * NB

    @pl.loop(start_upper, solved.shape[0])
    def _(index):
        solved[index] = jnp.zeros((sc, BS), jnp.float32)

    def live_rows(node, h):
        lanes = lax.broadcasted_iota(jnp.int32, (sc, BS), 1) + (r * rows_s + h * BS)
        return lanes < order_s[node]

    def copy(src, dst, ssem, rsem, dev):
        return pltpu.make_async_remote_copy(
            src_ref=src,
            dst_ref=dst,
            send_sem=ssem,
            recv_sem=rsem,
            device_id=dev,
            device_id_type=pl.DeviceIdType.MESH,
        )

    def guard(cond, go):
        go() if cond is None else pl.when(cond)(go)

    def both_of(first_cond, second_cond):
        if first_cond is None:
            return second_cond
        return first_cond if second_cond is None else first_cond & second_cond

    def send(cond, src, dst, ssem, rsem, dev):
        guard(cond, lambda: copy(src, dst, ssem, rsem, dev).start())

    def arrived(cond, piece, sem):
        guard(cond, lambda: copy(piece, piece, sem, sem, (r, c)).wait_recv())

    def landed(cond, count, sem):
        arrived(cond, solved.at[pl.ds(0, count)], sem)

    waits = []

    def sent(cond, count, sem):
        def go():
            piece = solved.at[pl.ds(0, count)]
            copy(piece, piece, sem, sem, (r, c)).wait_send()

        waits.append((cond, go))

    def drain():
        for cond, go in waits:
            guard(cond, go)
        waits.clear()

    stores = []

    def run(level):
        first, members = layout[level]
        mh = members * hb
        base = first * NB
        pieces = PIECES[level]
        nodes = members // pieces
        size = nodes * hb
        own, relay, held, stage, terms, part, got, cross = [
            buffers[name][level]
            for name in ("own", "relay", "held", "stage", "terms", "part", "got", "cross")
        ]
        last = level == LEVELS - 1

        def rows(ch):
            return pl.ds(ch * size, size)

        def share(ch, to_z, to_x):
            return part.at[pl.ds(((ch * nx + to_x) * nz + to_z) * size, size)]

        def cross_send(ch):
            if TWO_STEP[level][ch]:
                send(
                    None,
                    part.at[pl.ds((ch * nx + 1 - x) * nz * size, nz * size)],
                    cross.at[ch],
                    x_send.at[ch],
                    x_recv.at[ch],
                    (beside, c),
                )
                sent(None, nz * size, x_send.at[ch])
                return
            for d in range(1, ns):
                to = lax.rem(r + d, ns)
                send(
                    None,
                    share(ch, to // nx, to % nx),
                    got.at[ch, d - 1],
                    a_send.at[ch],
                    a_recv.at[ch],
                    (to, c),
                )
            sent(None, (ns - 1) * size, a_send.at[ch])

        def cross_sum(ch):
            if not TWO_STEP[level][ch]:
                return
            arrived(None, cross.at[ch], x_recv.at[ch])

            @pl.loop(0, nz * size)
            def _(i):
                spot = (ch * nx + x) * nz * size + i
                part[spot] = part[spot] + cross[ch, i]

            for d in range(1, nz):
                to = lax.rem(z + d, nz)
                send(
                    None,
                    share(ch, to, x),
                    got.at[ch, d - 1],
                    a_send.at[ch],
                    a_recv.at[ch],
                    (to * nx + x, c),
                )
            sent(None, (nz - 1) * size, a_send.at[ch])

        def own_rows(ch):
            others = nz - 1 if level and TWO_STEP[level][ch] else ns - 1
            if level:
                arrived(None, got.at[ch, pl.ds(0, others)], a_recv.at[ch])

            @pl.loop(0, nodes)
            def _(n):
                node = first + ch * nodes + n
                for h in range(hb):
                    i = n * hb + h
                    value = rhs_ref[node, :, h * BS : (h + 1) * BS]
                    if level:
                        value = value - part[((ch * nx + x) * nz + z) * size + i]
                        for d in range(others):
                            value = value - got[ch, d, i]
                    own[ch * size + i] = jnp.where(live_rows(node, h), value, 0.0)

        def spread(cond, zs, source, ch):
            slot = x * nc + c
            for way, to in enumerate((r, beside)):
                send(
                    both_of(cond, c != zs) if way == 0 else cond,
                    source.at[rows(ch)],
                    held.at[slot, rows(ch)],
                    s_send.at[ch],
                    s_recv.at[ch],
                    (to, zs),
                )

            @pl.when(both_of(cond, c == zs))
            def _():
                @pl.loop(ch * size, (ch + 1) * size)
                def _(i):
                    held[slot, i] = source[i]

        def climb(cond, zs, source, ch, d):
            send(
                both_of(cond, z + d < nz),
                source.at[rows(ch)],
                relay.at[zs, rows(ch)],
                b_send.at[ch],
                b_recv.at[ch, zs],
                (r + nx * d, c),
            )

        def start_rows(ch):
            for d in range(1, 2 if CHAIN[level][ch] else nz):
                climb(None, z, own, ch, d)
            if level:
                spread(None, z, own, ch)
            for t in range(nz):
                climbs = (t + 1 if t < nz - 1 else 0) if CHAIN[level][ch] else nz - 1 - t
                if climbs:
                    sent(z == t, climbs * size, b_send.at[ch])
                sent((z == t) & active, (2 * t + 1) * size, s_send.at[ch])
                if t < nz - 1:
                    sent((z == t) & (c > z), (2 * t + 2) * size, s_send.at[ch])

        def pass_rows(ch):
            for d in range(1, nz):
                zs = jnp.maximum(z - d, 0)
                arrived(z >= d, relay.at[zs, rows(ch)], b_recv.at[ch, zs])
                if CHAIN[level][ch]:
                    climb(z >= d, zs, relay.at[zs], ch, 1)
                spread(z >= d, zs, relay.at[zs], ch)
            if level == 0:
                spread(None, z, own, ch)

        def product(ch):
            landed(active, (ns - 1) * size, s_recv.at[ch])

            @pl.when(active)
            def _():
                @pl.loop(ch * nodes, (ch + 1) * nodes)
                def _(n):
                    columns = []
                    for qi in range(nx):
                        for h in range(hb):
                            columns.append(
                                jnp.concatenate(
                                    [held[qi * nc + c2, n * hb + h] for c2 in range(nc)], axis=0
                                )
                            )
                    high, low = split(jnp.concatenate(columns, axis=1))
                    right_h = inv_h[first + n]
                    right_l = inv_l[first + n]
                    value = dot_nt(high, right_h) + (dot_nt(low, right_h) + dot_nt(high, right_l))
                    for c2 in range(nc):
                        for h in range(hb):
                            stage[c2, n * hb + h] = value[
                                c2 * sc : (c2 + 1) * sc, h * BS : (h + 1) * BS
                            ]
                    for h in range(hb):
                        terms[c, n * hb + h] = stage[c, n * hb + h]

            for d in range(1, nc):
                to = lax.rem(c + d, nc)
                send(
                    active,
                    stage.at[to, rows(ch)],
                    terms.at[c, rows(ch)],
                    c_send.at[ch],
                    c_recv.at[ch],
                    (r, to),
                )
            sent(active, (nc - 1) * size, c_send.at[ch])

        def rows_of(rs, ch):
            return solved.at[pl.ds(base + rs * mh + ch * size, size)]

        def gather(cond, rs, ch, to, place=None):
            place = rs // nx if place is None else place
            send(
                cond,
                rows_of(rs, ch),
                rows_of(rs, ch),
                d_send.at[ch],
                d_recv.at[ch, place],
                (to, c),
            )

        def collect(ch):
            for t in range(nz):
                if t:
                    landed((z == t) & active, t * size, c_recv.at[ch])
                if t < nz - 1:
                    landed((z == t) & (c > z), (t + 1) * size, c_recv.at[ch])
            for t in range(nz):

                @pl.when(z == t)
                def _(t=t):
                    @pl.loop(ch * nodes, (ch + 1) * nodes)
                    def _(n):
                        for h in range(hb):
                            i = n * hb + h
                            value = terms[0, i]
                            for c2 in range(1, t + 1):
                                value = value + terms[c2, i]
                            value = jnp.where(live_rows(first + n, h), value, 0.0)
                            out_v[first + n, :, h * BS : (h + 1) * BS] = value
                            if not last:
                                solved[base + r * mh + i] = value

            if last:
                return
            if CHAIN_BACK[level][ch]:
                gather(above, r, ch, r + nx)
                gather(below, r, ch, r - nx)
            else:
                for d in range(1, nz):
                    gather(None, r, ch, lax.rem(z + d, nz) * nx + x)
            gather(None, r, ch, beside, nz)

        def pass_one(ch, step, d, cond=None):
            there = both_of(cond, z >= d if step < 0 else z + d < nz)
            rs = r + step * d * nx
            arrived(there, rows_of(rs, ch), d_recv.at[ch, rs // nx])
            if CHAIN_BACK[level][ch]:
                gather(there & (above if step < 0 else below), rs, ch, r - step * nx)
            gather(there, rs, ch, beside, nz)

        def pass_lower(ch):
            for d in range(1, nz):
                pass_one(ch, -1, d)

        early = range(2 if pieces > 2 else 0)

        def pass_early(ch):
            if ch in early:
                pass_one(ch, 1, 1, z == nz - 2)

        def pass_upper():
            order = [(2 * ch + LAG * (d - 1), d, ch) for ch in range(pieces) for d in range(1, nz)]
            for _, d, ch in sorted(order):
                pass_one(ch, 1, d, z < nz - 2 if d == 1 and ch in early else None)
            for ch in range(pieces):
                if CHAIN_BACK[level][ch]:
                    sent(above & below, (2 * nz + 1) * size, d_send.at[ch])
                    sent((z == 0) | (z == nz - 1), (nz + 1) * size, d_send.at[ch])
                else:
                    sent(None, (2 * nz - 1) * size, d_send.at[ch])

        stages = [own_rows_and_start(own_rows, start_rows), pass_rows, product, collect]
        if level:
            for ch in range(pieces):
                cross_send(ch)
            stages.insert(0, cross_sum)
        else:
            for ch in range(pieces):
                own_rows(ch)
                if ch == 0:
                    pl.semaphore_wait(barrier, len(partners))
                start_rows(ch)
            stages.pop(0)
        if not last:
            stages.append(pass_lower)
        for t in range(pieces + len(stages) - 1):
            if level == 0 and t == 0:
                load_a.wait()

                @pl.when(active)
                def _():
                    split_inverse(inv_f, inv_h, inv_l, 0, low_nodes)

            if level == 0 and t == 1:
                make_selection(parent_s, row_v, col_v, sel, layout, hb, ns // nc, nc)
                load_c.wait()
                load_b.wait()

                @pl.when(active)
                def _():
                    split_inverse(inv_f, inv_h, inv_l, low_nodes, total)

            passed = t - stages.index(collect)
            if passed == 2:
                pass_early(0)
            for s, one in enumerate(stages):
                if 0 <= t - s < pieces:
                    one(t - s)
            if passed == 3:
                pass_early(1)
        if level == 0:
            turn_blocks(z == 0)
        if not last:
            pass_upper()
        if level == 0:
            turn_blocks(z > 0)
        store = pltpu.make_async_copy(
            out_v.at[pl.ds(first, members)],
            out_hbm.at[pl.ds(first, members)],
            store_sem.at[level],
        )
        store.start()
        stores.append(store)
        if not last:
            for ch in range(pieces):
                landed(None, nz * size, d_recv.at[ch, nz])

    def turn_blocks(cond):
        @pl.when(cond)
        def _():
            @pl.loop(0, slots, unroll=4)
            def _(k):
                high, low = split(jnp.transpose(fac_f[k]))
                fac_w[k, 0:BS, :] = high
                fac_w[k, BS : 2 * BS, :] = low

    def update(level):
        first, members = layout[level]
        part = buffers["part"][level]

        def one_block(k, carry):
            block = col_s[k]
            node = block // NB
            inside = block % NB
            offset = jnp.int32(0)
            count = jnp.int32(layout[0][1])
            for begin, many in layout[1:-1]:
                over = node >= begin
                offset = jnp.where(over, begin, offset)
                count = jnp.where(over, many, count)
            index = (
                offset * NB
                + (inside // hb) * (count * hb)
                + (node - offset) * hb
                + inside % hb
            )
            high, low = split(solved[index])
            left = jnp.concatenate(
                [
                    jnp.concatenate([high, high], axis=1),
                    jnp.concatenate([low, jnp.zeros_like(low)], axis=1),
                ],
                axis=0,
            )
            both = jnp.dot(left, fac_w[k], preferred_element_type=jnp.float32)
            upd[pl.ds(pl.multiple_of(k * sc, sc), sc), :] = both[:sc] + both[sc:]
            return carry

        lax.fori_loop(0, slots, one_block, 0, unroll=slots // 2)

        sel_first = (first - low_nodes) * NB
        picked = sel[sel_first : sel_first + members * NB, :]
        for s in range(0, sc, 2):
            pair = jnp.concatenate(
                [upd[pl.ds(s + t, slots, stride=sc), :] for t in range(2)], axis=1
            )
            summed = jnp.dot(
                picked,
                jnp.concatenate(split(pair), axis=0),
                preferred_element_type=jnp.float32,
            )
            for t in range(2):
                part.reshape(members * NB * sc, BS)[
                    pl.ds(s + t, members * NB, stride=sc), :
                ] = summed[:, t * BS : (t + 1) * BS]

    for level in range(LEVELS):
        if level:
            update(level)
            drain()
        run(level)
    for store in stores:
        store.wait()
    drain()


def own_rows_and_start(own_rows, start_rows):
    def go(ch):
        own_rows(ch)
        start_rows(ch)

    return go


def split_inverse(inv_f, inv_h, inv_l, begin, stop):
    chunk = 32
    rows = inv_f.shape[1]

    @pl.loop(begin, stop)
    def _(n):
        @pl.loop(0, rows // chunk)
        def _(i):
            part = pl.ds(pl.multiple_of(i * chunk, chunk), chunk)
            high, low = split(inv_f[n, part, :])
            inv_h[n, part, :] = high
            inv_l[n, part, :] = low


def make_selection(parent_s, row_v, col_v, sel, layout, hb, nx, nz):
    row_block = row_v[...]
    row_node = row_block // NB
    walker = col_v[...] // NB
    valid = jnp.zeros(walker.shape, jnp.bool_)
    nodes = layout[-1][0] + 1
    for repeat in range(LEVELS - 1):
        moved = jnp.zeros_like(walker)
        for t in range(nodes):
            moved = jnp.where(walker == t, parent_s[t], moved)
        walker = moved
        valid = valid | (walker == row_node)
    inside = row_block % NB
    place = jnp.full(row_block.shape, -1, jnp.int32)
    low_nodes = layout[0][1]
    holder = inside // hb
    for level in range(1, LEVELS):
        begin, many = layout[level]
        nodes = many // PIECES[level]
        chunk = (row_node - begin) // nodes
        spot = (
            (begin - low_nodes) * NB
            + ((chunk * nx + holder % nx) * nz + holder // nx) * (nodes * hb)
            + (row_node - begin - chunk * nodes) * hb
            + inside % hb
        )
        place = jnp.where(row_node >= begin, spot, place)
    place = jnp.where(valid, place, -1)
    count, slots = sel.shape[0], row_block.shape[1]
    rows = lax.broadcasted_iota(jnp.int32, (count, slots), 0)
    hits = rows == jnp.broadcast_to(place, (count, slots))
    once = jnp.where(hits, 1.0, 0.0).astype(jnp.bfloat16)
    sel[...] = jnp.concatenate([once, once], axis=1)


def fused_device(
    ns, nc, right_side, inverse_diag, factor_blocks, parent, node_order, block_row, block_col
):
    total, sc, rows_s = right_side.shape
    columns = inverse_diag.shape[2]
    slots = factor_blocks.shape[0]
    hb = rows_s // BS
    layout = level_layout()
    f32, bf16 = jnp.float32, jnp.bfloat16
    upper = total - layout[0][1]


    def per_level(lead, skip=0):
        return [pltpu.VMEM((*lead, m * hb, sc, BS), f32) for _, m in layout[skip:]]

    def per_piece(lead):
        return [
            pltpu.VMEM((PIECES[k], *lead(k, layout[k][1] // PIECES[k] * hb), sc, BS), f32)
            for k in range(1, LEVELS)
        ]

    sems = pltpu.SemaphoreType.DMA
    most = max(PIECES)
    scratch = [
        pltpu.VMEM((total, rows_s, columns), f32),
        pltpu.VMEM((total, rows_s, columns), bf16),
        pltpu.VMEM((total, rows_s, columns), bf16),
        pltpu.VMEM((slots, BS, BS), f32),
        pltpu.VMEM((slots, 2 * BS, BS), bf16),
        pltpu.VMEM((slots * sc, BS), f32),
        pltpu.VMEM((upper * NB, 2 * slots), bf16),
        pltpu.VMEM(((total - 1) * NB, sc, BS), f32),
        pltpu.VMEM(right_side.shape, f32),
        *per_level(()),
        *per_level((nc - 1,)),
        *per_level((ns,)),
        *per_level((nc,)),
        *per_level((nc,)),
        *[pltpu.VMEM((m * NB, sc, BS), f32) for _, m in layout[1:]],
        *per_piece(lambda k, size: (ns - 1, size)),
        *per_piece(lambda k, size: (nc * size,)),
        sems((3,)),
        sems((LEVELS,)),
        sems((most,)),
        sems((most,)),
        sems((most,)),
        sems((most,)),
        sems((most,)),
        sems((most, nc - 1)),
        sems((most,)),
        sems((most,)),
        sems((most,)),
        sems((most,)),
        sems((most,)),
        sems((most, nc + 1)),
    ]
    smem = pl.BlockSpec(memory_space=pltpu.SMEM)
    vmem = pl.BlockSpec(memory_space=pltpu.VMEM)
    hbm = pl.BlockSpec(memory_space=pl.ANY)
    return pl.pallas_call(
        functools.partial(kernel, ns, nc),
        out_shape=jax.ShapeDtypeStruct(right_side.shape, f32),
        in_specs=[smem, smem, smem, vmem, vmem, vmem, hbm, hbm],
        out_specs=hbm,
        scratch_shapes=scratch,
        compiler_params=pltpu.CompilerParams(
            collective_id=0, has_side_effects=True, vmem_limit_bytes=60 * 2**20
        ),
        name="substitute",
    )(
        parent,
        node_order,
        block_col,
        right_side,
        block_row[None, :],
        block_col[None, :],
        inverse_diag,
        factor_blocks,
    )


def solution(mesh):
    ns, nc = mesh.shape["sn"], mesh.shape["rhs"]
    in_specs = (
        P(None, "rhs", "sn"),
        P(None, "sn", "rhs"),
        P("sn", None, None),
        P(),
        P(),
        P("sn"),
        P("sn"),
    )
    out_specs = P(None, "rhs", "sn")
    fused = S % (ns * BS) == 0 and ns == 2 * nc and nc == 4
    body = functools.partial(fused_device, ns, nc) if fused else per_device
    return jax.shard_map(
        body, mesh=mesh, in_specs=in_specs, out_specs=out_specs, check_vma=False
    )
```

```python
import functools

import jax
import jax.numpy as jnp
from jax import lax
from jax.experimental import pallas as pl
from jax.experimental.pallas import tpu as pltpu
from jax.sharding import PartitionSpec as P

S = 2048
BS = 128
NB = 16
LEVELS = 4
PIECES = (4, 4, 2, 1)
CHAIN = ((False, True, True, True), (False, True, True, True), (False,) * 4, (False, False))
LAG = 1
CHAIN_BACK = ((True, True, True, True), (True, True, True, True), (False, False))
SUB = (1, 1, 2, 2)
TWO_STEP = (None, (True, True, True, False), (False, True, True, False), (False, False))
BUFFERS = (
    ("own", 0),
    ("relay", 0),
    ("held", 0),
    ("stage", 0),
    ("terms", 0),
    ("part", 1),
    ("got", 1),
    ("cross", 1),
)


def level_layout():
    layout = []
    offset_value = 0
    for level_index in range(LEVELS):
        members = 2 ** (LEVELS - 1 - level_index)
        layout.append((offset_value, members))
        offset_value += members
    return layout


def to_blocks(values):
    count, scen_count, rows_total = values.shape
    return jnp.transpose(values.reshape(count, scen_count, NB, BS), (0, 2, 1, 3)).reshape(
        count * NB, scen_count, BS
    )


def from_blocks(values):
    count = values.shape[0] // NB
    scen_count = values.shape[1]
    return jnp.transpose(values.reshape(count, NB, scen_count, BS), (0, 2, 1, 3)).reshape(
        count, scen_count, NB * BS
    )


def table_lookup(table, index_values):
    hits = index_values[:, None] == jnp.arange(table.shape[0], dtype=jnp.int32)[None, :]
    return jnp.sum(jnp.where(hits, table[None, :], 0), axis=1)


def per_device(right_side, inverse_diag, factor_blocks, parent, node_order, block_row, block_col):
    node_total, sc_dev, rows_s = right_side.shape
    layout = level_layout()
    col_node = block_col // NB
    row_node = block_row // NB
    walker = col_node
    valid = jnp.zeros(col_node.shape, dtype=bool)
    for repeat in range(LEVELS - 1):
        walker = table_lookup(parent, walker)
        valid = valid | (walker == row_node)
    col_level = jnp.zeros(col_node.shape, jnp.int32)
    for level_index in range(1, LEVELS):
        col_level = col_level + (col_node >= layout[level_index][0]).astype(jnp.int32)
    own_offset = lax.axis_index("sn") * rows_s
    live = (jnp.arange(S, dtype=jnp.int32)[None, :] < node_order[:, None]).astype(jnp.float32)
    own_rows = own_offset + jnp.arange(rows_s, dtype=jnp.int32)
    live_own = (own_rows[None, :] < node_order[:, None]).astype(jnp.float32)
    partial_blocks = jnp.zeros((node_total * NB, sc_dev, BS), jnp.float32)
    solved_blocks = jnp.zeros((node_total * NB, sc_dev, BS), jnp.float32)
    pieces_out = []
    for level_index in range(LEVELS):
        first_node, members = layout[level_index]
        stop_node = first_node + members
        placed = lax.dynamic_update_slice_in_dim(
            jnp.zeros((members, sc_dev, S), jnp.float32),
            right_side[first_node:stop_node],
            own_offset,
            2,
        )
        r_term = placed - from_blocks(partial_blocks[first_node * NB : stop_node * NB])
        r_full = lax.psum(r_term, "sn")
        masked = r_full * live[first_node:stop_node, None, :]
        moved = lax.all_to_all(masked, "rhs", split_axis=2, concat_axis=1, tiled=True)
        block_inverse = inverse_diag[first_node:stop_node]

        def inverse_term(offset, length, moved=moved, block_inverse=block_inverse):
            return jnp.einsum("ncj,nij->cni", moved, block_inverse, precision=lax.Precision.HIGHEST)

        summed = lax.psum_scatter(
            inverse_term(jnp.int32(0), sc_dev * lax.axis_size("rhs")),
            "rhs",
            scatter_dimension=0,
            tiled=True,
        )
        y_piece = jnp.transpose(summed, (1, 0, 2))
        y_piece = y_piece * live_own[first_node:stop_node, None, :]
        pieces_out.append(y_piece)
        if level_index < LEVELS - 1:
            gathered = lax.all_gather(y_piece, "sn", axis=2, tiled=True)
            solved_blocks = solved_blocks.at[first_node * NB : stop_node * NB].set(
                to_blocks(gathered)
            )
            weights = (valid & (col_level == level_index)).astype(jnp.float32)
            columns = lax.map(
                lambda block, source=solved_blocks: lax.dynamic_index_in_dim(
                    source, block, 0, keepdims=False
                ),
                block_col,
            )
            update_terms = jnp.einsum(
                "kij,kcj->kci", factor_blocks, columns, precision=lax.Precision.HIGHEST
            )
            update_terms = update_terms * weights[:, None, None]
            partial_blocks = partial_blocks.at[block_row].add(update_terms)
    return jnp.concatenate(pieces_out, axis=0)


def split(values):
    high = values.astype(jnp.bfloat16)
    low = (values - high.astype(jnp.float32)).astype(jnp.bfloat16)
    return high, low


def dot_nt(left, right):
    return lax.dot_general(
        left, right, (((1,), (1,)), ((), ())), preferred_element_type=jnp.float32
    )


def kernel(
    ns,
    nc,
    parent_s,
    order_s,
    col_s,
    rhs_ref,
    row_v,
    col_v,
    inv_hbm,
    fac_hbm,
    out_hbm,
    *scratch,
):
    layout = level_layout()
    names = iter(scratch)
    inv_f, inv_h, inv_l, fac_f, fac_w, upd, sel, solved, out_v = [next(names) for _ in range(9)]
    buffers = {}
    for name, skip in BUFFERS:
        buffers[name] = [None] * skip + [next(names) for _ in layout[skip:]]
    load_sem, store_sem = next(names), next(names)
    x_send, x_recv, a_send, a_recv, b_send, b_recv, s_send, s_recv, c_send, c_recv, d_send, d_recv = [
        next(names) for _ in range(12)
    ]

    r = lax.axis_index("sn")
    c = lax.axis_index("rhs")
    nz, nx = nc, ns // nc
    z = r // nx
    x = r % nx
    active = c <= z
    above = z < nz - 1
    below = z > 0
    beside = r + 1 - 2 * x
    slots = fac_f.shape[0]
    sc = rhs_ref.shape[1]
    rows_s = rhs_ref.shape[2]
    hb = rows_s // BS
    low_nodes = layout[0][1]
    total = inv_f.shape[0]

    load_a = pltpu.make_async_copy(
        inv_hbm.at[pl.ds(0, low_nodes)], inv_f.at[pl.ds(0, low_nodes)], load_sem.at[0]
    )
    load_b = pltpu.make_async_copy(
        inv_hbm.at[pl.ds(low_nodes, total - low_nodes)],
        inv_f.at[pl.ds(low_nodes, total - low_nodes)],
        load_sem.at[1],
    )
    load_c = pltpu.make_async_copy(fac_hbm, fac_f, load_sem.at[2])
    load_a.start()
    load_c.start()
    load_b.start()

    barrier = pltpu.get_barrier_semaphore()
    partners = [(lax.rem(r + d, ns), c) for d in range(1, ns)]
    for dx in range(nx):
        for dc in range(1, nc):
            partners.append((z * nx + lax.rem(x + dx, nx), lax.rem(c + dc, nc)))
    for partner in partners:
        pl.semaphore_signal(
            barrier, inc=1, device_id=partner, device_id_type=pl.DeviceIdType.MESH
        )

    start_upper = low_nodes * NB

    @pl.loop(start_upper, solved.shape[0])
    def _(index):
        solved[index] = jnp.zeros((sc, BS), jnp.float32)

    def live_rows(node, h):
        lanes = lax.broadcasted_iota(jnp.int32, (sc, BS), 1) + (r * rows_s + h * BS)
        return lanes < order_s[node]

    def copy(src, dst, ssem, rsem, dev):
        return pltpu.make_async_remote_copy(
            src_ref=src,
            dst_ref=dst,
            send_sem=ssem,
            recv_sem=rsem,
            device_id=dev,
            device_id_type=pl.DeviceIdType.MESH,
        )

    def guard(cond, go):
        go() if cond is None else pl.when(cond)(go)

    def both_of(first_cond, second_cond):
        if first_cond is None:
            return second_cond
        return first_cond if second_cond is None else first_cond & second_cond

    def send(cond, src, dst, ssem, rsem, dev):
        guard(cond, lambda: copy(src, dst, ssem, rsem, dev).start())

    def arrived(cond, piece, sem):
        guard(cond, lambda: copy(piece, piece, sem, sem, (r, c)).wait_recv())

    def landed(cond, count, sem):
        arrived(cond, solved.at[pl.ds(0, count)], sem)

    waits = []

    def sent(cond, count, sem):
        def go():
            piece = solved.at[pl.ds(0, count)]
            copy(piece, piece, sem, sem, (r, c)).wait_send()

        waits.append((cond, go))

    def drain():
        for cond, go in waits:
            guard(cond, go)
        waits.clear()

    stores = []

    def run(level):
        first, members = layout[level]
        mh = members * hb
        base = first * NB
        pieces = PIECES[level]
        nodes = members // pieces
        size = nodes * hb
        own, relay, held, stage, terms, part, got, cross = [
            buffers[name][level]
            for name in ("own", "relay", "held", "stage", "terms", "part", "got", "cross")
        ]
        last = level == LEVELS - 1
        fine = pieces * SUB[level]
        fsize = size // SUB[level]

        def rows(ch):
            return pl.ds(ch * size, size)

        def fine_rows(ch):
            return pl.ds(ch * fsize, fsize)

        def share(ch, to_z, to_x):
            return part.at[pl.ds(((ch * nx + to_x) * nz + to_z) * fsize, fsize)]

        def cross_send(ch):
            if TWO_STEP[level][ch]:
                send(
                    None,
                    part.at[pl.ds((ch * nx + 1 - x) * nz * fsize, nz * fsize)],
                    cross.at[ch],
                    x_send.at[ch],
                    x_recv.at[ch],
                    (beside, c),
                )
                sent(None, nz * fsize, x_send.at[ch])
                return
            for d in range(1, ns):
                to = lax.rem(r + d, ns)
                send(
                    None,
                    share(ch, to // nx, to % nx),
                    got.at[ch, d - 1],
                    a_send.at[ch],
                    a_recv.at[ch],
                    (to, c),
                )
            sent(None, (ns - 1) * fsize, a_send.at[ch])

        def cross_sum(ch):
            if not TWO_STEP[level][ch]:
                return
            arrived(None, cross.at[ch], x_recv.at[ch])

            @pl.loop(0, nz * fsize)
            def _(i):
                spot = (ch * nx + x) * nz * fsize + i
                part[spot] = part[spot] + cross[ch, i]

            for d in range(1, nz):
                to = lax.rem(z + d, nz)
                send(
                    None,
                    share(ch, to, x),
                    got.at[ch, d - 1],
                    a_send.at[ch],
                    a_recv.at[ch],
                    (to * nx + x, c),
                )
            sent(None, (nz - 1) * fsize, a_send.at[ch])

        def own_rows(ch):
            others = nz - 1 if level and TWO_STEP[level][ch] else ns - 1
            if level:
                arrived(None, got.at[ch, pl.ds(0, others)], a_recv.at[ch])

            def one_row(i, node, h):
                value = rhs_ref[node, :, h * BS : (h + 1) * BS]
                if level:
                    value = value - part[((ch * nx + x) * nz + z) * fsize + i]
                    for d in range(others):
                        value = value - got[ch, d, i]
                own[ch * fsize + i] = jnp.where(live_rows(node, h), value, 0.0)

            if fsize < hb:
                one_row(0, first + ch // hb, ch % hb)
                return

            @pl.loop(0, nodes)
            def _(n):
                for h in range(hb):
                    one_row(n * hb + h, first + ch * nodes + n, h)

        def spread(cond, zs, source, ch):
            slot = x * nc + c
            for way, to in enumerate((r, beside)):
                send(
                    both_of(cond, c != zs) if way == 0 else cond,
                    source.at[fine_rows(ch)],
                    held.at[slot, fine_rows(ch)],
                    s_send.at[ch],
                    s_recv.at[ch],
                    (to, zs),
                )

            @pl.when(both_of(cond, c == zs))
            def _():
                @pl.loop(ch * fsize, (ch + 1) * fsize)
                def _(i):
                    held[slot, i] = source[i]

        def climb(cond, zs, source, ch, d):
            send(
                both_of(cond, z + d < nz),
                source.at[fine_rows(ch)],
                relay.at[zs, fine_rows(ch)],
                b_send.at[ch],
                b_recv.at[ch, zs],
                (r + nx * d, c),
            )

        def start_rows(ch):
            for d in range(1, 2 if CHAIN[level][ch] else nz):
                climb(None, z, own, ch, d)
            if level:
                spread(None, z, own, ch)
            for t in range(nz):
                climbs = (t + 1 if t < nz - 1 else 0) if CHAIN[level][ch] else nz - 1 - t
                if climbs:
                    sent(z == t, climbs * fsize, b_send.at[ch])
                sent((z == t) & active, (2 * t + 1) * fsize, s_send.at[ch])
                if t < nz - 1:
                    sent((z == t) & (c > z), (2 * t + 2) * fsize, s_send.at[ch])

        def pass_rows(ch):
            for d in range(1, nz):
                zs = jnp.maximum(z - d, 0)
                arrived(z >= d, relay.at[zs, fine_rows(ch)], b_recv.at[ch, zs])
                if CHAIN[level][ch]:
                    climb(z >= d, zs, relay.at[zs], ch, 1)
                spread(z >= d, zs, relay.at[zs], ch)
            if level == 0:
                spread(None, z, own, ch)

        def product(ch):
            for f in range(ch * SUB[level], (ch + 1) * SUB[level]):
                landed(active, (ns - 1) * fsize, s_recv.at[f])

            @pl.when(active)
            def _():
                @pl.loop(ch * nodes, (ch + 1) * nodes)
                def _(n):
                    columns = []
                    for qi in range(nx):
                        for h in range(hb):
                            columns.append(
                                jnp.concatenate(
                                    [held[qi * nc + c2, n * hb + h] for c2 in range(nc)], axis=0
                                )
                            )
                    high, low = split(jnp.concatenate(columns, axis=1))
                    right_h = inv_h[first + n]
                    right_l = inv_l[first + n]
                    value = dot_nt(high, right_h) + (dot_nt(low, right_h) + dot_nt(high, right_l))
                    for c2 in range(nc):
                        for h in range(hb):
                            stage[c2, n * hb + h] = value[
                                c2 * sc : (c2 + 1) * sc, h * BS : (h + 1) * BS
                            ]
                    for h in range(hb):
                        terms[c, n * hb + h] = stage[c, n * hb + h]

            for d in range(1, nc):
                to = lax.rem(c + d, nc)
                send(
                    active,
                    stage.at[to, rows(ch)],
                    terms.at[c, rows(ch)],
                    c_send.at[ch],
                    c_recv.at[ch],
                    (r, to),
                )
            sent(active, (nc - 1) * size, c_send.at[ch])

        def rows_of(rs, ch):
            return solved.at[pl.ds(base + rs * mh + ch * size, size)]

        def gather(cond, rs, ch, to, place=None):
            place = rs // nx if place is None else place
            send(
                cond,
                rows_of(rs, ch),
                rows_of(rs, ch),
                d_send.at[ch],
                d_recv.at[ch, place],
                (to, c),
            )

        def collect(ch):
            for t in range(nz):
                if t:
                    landed((z == t) & active, t * size, c_recv.at[ch])
                if t < nz - 1:
                    landed((z == t) & (c > z), (t + 1) * size, c_recv.at[ch])
            for t in range(nz):

                @pl.when(z == t)
                def _(t=t):
                    @pl.loop(ch * nodes, (ch + 1) * nodes)
                    def _(n):
                        for h in range(hb):
                            i = n * hb + h
                            value = terms[0, i]
                            for c2 in range(1, t + 1):
                                value = value + terms[c2, i]
                            value = jnp.where(live_rows(first + n, h), value, 0.0)
                            out_v[first + n, :, h * BS : (h + 1) * BS] = value
                            if not last:
                                solved[base + r * mh + i] = value

            if last:
                return
            if CHAIN_BACK[level][ch]:
                gather(above, r, ch, r + nx)
                gather(below, r, ch, r - nx)
            else:
                for d in range(1, nz):
                    gather(None, r, ch, lax.rem(z + d, nz) * nx + x)
            gather(None, r, ch, beside, nz)

        def pass_one(ch, step, d, cond=None):
            there = both_of(cond, z >= d if step < 0 else z + d < nz)
            rs = r + step * d * nx
            arrived(there, rows_of(rs, ch), d_recv.at[ch, rs // nx])
            if CHAIN_BACK[level][ch]:
                gather(there & (above if step < 0 else below), rs, ch, r - step * nx)
            gather(there, rs, ch, beside, nz)

        def pass_lower(ch):
            for d in range(1, nz):
                pass_one(ch, -1, d)

        early = range(2 if pieces > 2 else 0)

        def pass_early(ch):
            if ch in early:
                pass_one(ch, 1, 1, z == nz - 2)

        def pass_upper():
            order = [(2 * ch + LAG * (d - 1), d, ch) for ch in range(pieces) for d in range(1, nz)]
            for _, d, ch in sorted(order):
                pass_one(ch, 1, d, z < nz - 2 if d == 1 and ch in early else None)
            for ch in range(pieces):
                if CHAIN_BACK[level][ch]:
                    sent(above & below, (2 * nz + 1) * size, d_send.at[ch])
                    sent((z == 0) | (z == nz - 1), (nz + 1) * size, d_send.at[ch])
                else:
                    sent(None, (2 * nz - 1) * size, d_send.at[ch])

        stages = [own_rows_and_start(own_rows, start_rows), pass_rows, product, collect]
        if level:
            for ch in range(fine):
                cross_send(ch)
            stages.insert(0, cross_sum)
        else:
            for ch in range(pieces):
                own_rows(ch)
                if ch == 0:
                    pl.semaphore_wait(barrier, len(partners))
                start_rows(ch)
            stages.pop(0)
        if not last:
            stages.append(pass_lower)
        whole = (product, collect, pass_lower)
        for t in range(fine + len(stages) - 1):
            if level == 0 and t == 0:
                load_a.wait()

                @pl.when(active)
                def _():
                    split_inverse(inv_f, inv_h, inv_l, 0, low_nodes)

            if level == 0 and t == 1:
                make_selection(parent_s, row_v, col_v, sel, layout, hb, ns // nc, nc)
                load_c.wait()
                load_b.wait()

                @pl.when(active)
                def _():
                    split_inverse(inv_f, inv_h, inv_l, low_nodes, total)

            passed = t - stages.index(collect)
            if passed == 2:
                pass_early(0)
            for s, one in enumerate(stages):
                count = SUB[level] if one in whole else 1
                step = t - s + 1
                if step % count == 0 and 0 < step <= fine:
                    one(step // count - 1)
            if passed == 3:
                pass_early(1)
        if level == 0:
            turn_blocks(z == 0)
        if not last:
            pass_upper()
        if level == 0:
            turn_blocks(z > 0)
        store = pltpu.make_async_copy(
            out_v.at[pl.ds(first, members)],
            out_hbm.at[pl.ds(first, members)],
            store_sem.at[level],
        )
        store.start()
        stores.append(store)
        if not last:
            for ch in range(pieces):
                landed(None, nz * size, d_recv.at[ch, nz])

    def turn_blocks(cond):
        @pl.when(cond)
        def _():
            @pl.loop(0, slots, unroll=4)
            def _(k):
                high, low = split(jnp.transpose(fac_f[k]))
                fac_w[k, 0:BS, :] = high
                fac_w[k, BS : 2 * BS, :] = low

    def update(level):
        first, members = layout[level]
        part = buffers["part"][level]

        def one_block(k, carry):
            block = col_s[k]
            node = block // NB
            inside = block % NB
            offset = jnp.int32(0)
            count = jnp.int32(layout[0][1])
            for begin, many in layout[1:-1]:
                over = node >= begin
                offset = jnp.where(over, begin, offset)
                count = jnp.where(over, many, count)
            index = (
                offset * NB
                + (inside // hb) * (count * hb)
                + (node - offset) * hb
                + inside % hb
            )
            high, low = split(solved[index])
            left = jnp.concatenate(
                [
                    jnp.concatenate([high, high], axis=1),
                    jnp.concatenate([low, jnp.zeros_like(low)], axis=1),
                ],
                axis=0,
            )
            both = jnp.dot(left, fac_w[k], preferred_element_type=jnp.float32)
            upd[pl.ds(pl.multiple_of(k * sc, sc), sc), :] = both[:sc] + both[sc:]
            return carry

        lax.fori_loop(0, slots, one_block, 0, unroll=slots // 2)

        sel_first = (first - low_nodes) * NB
        picked = sel[sel_first : sel_first + members * NB, :]
        for s in range(0, sc, 2):
            pair = jnp.concatenate(
                [upd[pl.ds(s + t, slots, stride=sc), :] for t in range(2)], axis=1
            )
            summed = jnp.dot(
                picked,
                jnp.concatenate(split(pair), axis=0),
                preferred_element_type=jnp.float32,
            )
            for t in range(2):
                part.reshape(members * NB * sc, BS)[
                    pl.ds(s + t, members * NB, stride=sc), :
                ] = summed[:, t * BS : (t + 1) * BS]

    for level in range(LEVELS):
        if level:
            update(level)
            drain()
        run(level)
    for store in stores:
        store.wait()
    drain()


def own_rows_and_start(own_rows, start_rows):
    def go(ch):
        own_rows(ch)
        start_rows(ch)

    return go


def split_inverse(inv_f, inv_h, inv_l, begin, stop):
    chunk = 32
    rows = inv_f.shape[1]

    @pl.loop(begin, stop)
    def _(n):
        @pl.loop(0, rows // chunk)
        def _(i):
            part = pl.ds(pl.multiple_of(i * chunk, chunk), chunk)
            high, low = split(inv_f[n, part, :])
            inv_h[n, part, :] = high
            inv_l[n, part, :] = low


def make_selection(parent_s, row_v, col_v, sel, layout, hb, nx, nz):
    row_block = row_v[...]
    row_node = row_block // NB
    walker = col_v[...] // NB
    valid = jnp.zeros(walker.shape, jnp.bool_)
    nodes = layout[-1][0] + 1
    for repeat in range(LEVELS - 1):
        moved = jnp.zeros_like(walker)
        for t in range(nodes):
            moved = jnp.where(walker == t, parent_s[t], moved)
        walker = moved
        valid = valid | (walker == row_node)
    inside = row_block % NB
    place = jnp.full(row_block.shape, -1, jnp.int32)
    low_nodes = layout[0][1]
    holder = inside // hb
    for level in range(1, LEVELS):
        begin, many = layout[level]
        nodes = many // PIECES[level]
        chunk = (row_node - begin) // nodes
        spot = (
            (begin - low_nodes) * NB
            + ((chunk * nx + holder % nx) * nz + holder // nx) * (nodes * hb)
            + (row_node - begin - chunk * nodes) * hb
            + inside % hb
        )
        if SUB[level] > 1:
            chunk = (row_node - begin) * hb + inside % hb
            spot = (begin - low_nodes) * NB + (chunk * nx + holder % nx) * nz + holder // nx
        place = jnp.where(row_node >= begin, spot, place)
    place = jnp.where(valid, place, -1)
    count, slots = sel.shape[0], row_block.shape[1]
    rows = lax.broadcasted_iota(jnp.int32, (count, slots), 0)
    hits = rows == jnp.broadcast_to(place, (count, slots))
    once = jnp.where(hits, 1.0, 0.0).astype(jnp.bfloat16)
    sel[...] = jnp.concatenate([once, once], axis=1)


def fused_device(
    ns, nc, right_side, inverse_diag, factor_blocks, parent, node_order, block_row, block_col
):
    total, sc, rows_s = right_side.shape
    columns = inverse_diag.shape[2]
    slots = factor_blocks.shape[0]
    hb = rows_s // BS
    layout = level_layout()
    f32, bf16 = jnp.float32, jnp.bfloat16
    upper = total - layout[0][1]


    def per_level(lead, skip=0):
        return [pltpu.VMEM((*lead, m * hb, sc, BS), f32) for _, m in layout[skip:]]

    def per_piece(lead):
        return [
            pltpu.VMEM(
                (PIECES[k] * SUB[k], *lead(k, layout[k][1] * hb // PIECES[k] // SUB[k]), sc, BS), f32
            )
            for k in range(1, LEVELS)
        ]

    sems = pltpu.SemaphoreType.DMA
    most = max(count * sub for count, sub in zip(PIECES, SUB))
    scratch = [
        pltpu.VMEM((total, rows_s, columns), f32),
        pltpu.VMEM((total, rows_s, columns), bf16),
        pltpu.VMEM((total, rows_s, columns), bf16),
        pltpu.VMEM((slots, BS, BS), f32),
        pltpu.VMEM((slots, 2 * BS, BS), bf16),
        pltpu.VMEM((slots * sc, BS), f32),
        pltpu.VMEM((upper * NB, 2 * slots), bf16),
        pltpu.VMEM(((total - 1) * NB, sc, BS), f32),
        pltpu.VMEM(right_side.shape, f32),
        *per_level(()),
        *per_level((nc - 1,)),
        *per_level((ns,)),
        *per_level((nc,)),
        *per_level((nc,)),
        *[pltpu.VMEM((m * NB, sc, BS), f32) for _, m in layout[1:]],
        *per_piece(lambda k, size: (ns - 1, size)),
        *per_piece(lambda k, size: (nc * size,)),
        sems((3,)),
        sems((LEVELS,)),
        sems((most,)),
        sems((most,)),
        sems((most,)),
        sems((most,)),
        sems((most,)),
        sems((most, nc - 1)),
        sems((most,)),
        sems((most,)),
        sems((most,)),
        sems((most,)),
        sems((most,)),
        sems((most, nc + 1)),
    ]
    smem = pl.BlockSpec(memory_space=pltpu.SMEM)
    vmem = pl.BlockSpec(memory_space=pltpu.VMEM)
    hbm = pl.BlockSpec(memory_space=pl.ANY)
    return pl.pallas_call(
        functools.partial(kernel, ns, nc),
        out_shape=jax.ShapeDtypeStruct(right_side.shape, f32),
        in_specs=[smem, smem, smem, vmem, vmem, vmem, hbm, hbm],
        out_specs=hbm,
        scratch_shapes=scratch,
        compiler_params=pltpu.CompilerParams(
            collective_id=0, has_side_effects=True, vmem_limit_bytes=60 * 2**20
        ),
        name="substitute",
    )(
        parent,
        node_order,
        block_col,
        right_side,
        block_row[None, :],
        block_col[None, :],
        inverse_diag,
        factor_blocks,
    )


def solution(mesh):
    ns, nc = mesh.shape["sn"], mesh.shape["rhs"]
    in_specs = (
        P(None, "rhs", "sn"),
        P(None, "sn", "rhs"),
        P("sn", None, None),
        P(),
        P(),
        P("sn"),
        P("sn"),
    )
    out_specs = P(None, "rhs", "sn")
    fused = S == 2 * BS * ns and ns == 2 * nc and nc == 4
    body = functools.partial(fused_device, ns, nc) if fused else per_device
    return jax.shard_map(
        body, mesh=mesh, in_specs=in_specs, out_specs=out_specs, check_vma=False
    )
```

```python
import functools

import jax
import jax.numpy as jnp
from jax import lax
from jax.experimental import pallas as pl
from jax.experimental.pallas import tpu as pltpu
from jax.sharding import PartitionSpec as P

S = 2048
BS = 128
NB = 16
LEVELS = 4
PIECES = (4, 4, 2, 1)
CHAIN = ((False, True, True, True), (False, True, True, True), (False,) * 4, (False, False))
LAG = 1
CHAIN_BACK = ((True, True, True, True), (True, True, True, True), (False, False))
SUB = (1, 1, 2, 2)
TWO_STEP = (None, (True, True, True, False), (False, True, True, False), (False, False))
BUFFERS = (
    ("own", 0),
    ("relay", 0),
    ("held", 0),
    ("stage", 0),
    ("terms", 0),
    ("part", 1),
    ("got", 1),
    ("cross", 1),
)


def level_layout():
    layout = []
    offset_value = 0
    for level_index in range(LEVELS):
        members = 2 ** (LEVELS - 1 - level_index)
        layout.append((offset_value, members))
        offset_value += members
    return layout


def to_blocks(values):
    count, scen_count, rows_total = values.shape
    return jnp.transpose(values.reshape(count, scen_count, NB, BS), (0, 2, 1, 3)).reshape(
        count * NB, scen_count, BS
    )


def from_blocks(values):
    count = values.shape[0] // NB
    scen_count = values.shape[1]
    return jnp.transpose(values.reshape(count, NB, scen_count, BS), (0, 2, 1, 3)).reshape(
        count, scen_count, NB * BS
    )


def table_lookup(table, index_values):
    hits = index_values[:, None] == jnp.arange(table.shape[0], dtype=jnp.int32)[None, :]
    return jnp.sum(jnp.where(hits, table[None, :], 0), axis=1)


def per_device(right_side, inverse_diag, factor_blocks, parent, node_order, block_row, block_col):
    node_total, sc_dev, rows_s = right_side.shape
    layout = level_layout()
    col_node = block_col // NB
    row_node = block_row // NB
    walker = col_node
    valid = jnp.zeros(col_node.shape, dtype=bool)
    for repeat in range(LEVELS - 1):
        walker = table_lookup(parent, walker)
        valid = valid | (walker == row_node)
    col_level = jnp.zeros(col_node.shape, jnp.int32)
    for level_index in range(1, LEVELS):
        col_level = col_level + (col_node >= layout[level_index][0]).astype(jnp.int32)
    own_offset = lax.axis_index("sn") * rows_s
    live = (jnp.arange(S, dtype=jnp.int32)[None, :] < node_order[:, None]).astype(jnp.float32)
    own_rows = own_offset + jnp.arange(rows_s, dtype=jnp.int32)
    live_own = (own_rows[None, :] < node_order[:, None]).astype(jnp.float32)
    partial_blocks = jnp.zeros((node_total * NB, sc_dev, BS), jnp.float32)
    solved_blocks = jnp.zeros((node_total * NB, sc_dev, BS), jnp.float32)
    pieces_out = []
    for level_index in range(LEVELS):
        first_node, members = layout[level_index]
        stop_node = first_node + members
        placed = lax.dynamic_update_slice_in_dim(
            jnp.zeros((members, sc_dev, S), jnp.float32),
            right_side[first_node:stop_node],
            own_offset,
            2,
        )
        r_term = placed - from_blocks(partial_blocks[first_node * NB : stop_node * NB])
        r_full = lax.psum(r_term, "sn")
        masked = r_full * live[first_node:stop_node, None, :]
        moved = lax.all_to_all(masked, "rhs", split_axis=2, concat_axis=1, tiled=True)
        block_inverse = inverse_diag[first_node:stop_node]

        def inverse_term(offset, length, moved=moved, block_inverse=block_inverse):
            return jnp.einsum("ncj,nij->cni", moved, block_inverse, precision=lax.Precision.HIGHEST)

        summed = lax.psum_scatter(
            inverse_term(jnp.int32(0), sc_dev * lax.axis_size("rhs")),
            "rhs",
            scatter_dimension=0,
            tiled=True,
        )
        y_piece = jnp.transpose(summed, (1, 0, 2))
        y_piece = y_piece * live_own[first_node:stop_node, None, :]
        pieces_out.append(y_piece)
        if level_index < LEVELS - 1:
            gathered = lax.all_gather(y_piece, "sn", axis=2, tiled=True)
            solved_blocks = solved_blocks.at[first_node * NB : stop_node * NB].set(
                to_blocks(gathered)
            )
            weights = (valid & (col_level == level_index)).astype(jnp.float32)
            columns = lax.map(
                lambda block, source=solved_blocks: lax.dynamic_index_in_dim(
                    source, block, 0, keepdims=False
                ),
                block_col,
            )
            update_terms = jnp.einsum(
                "kij,kcj->kci", factor_blocks, columns, precision=lax.Precision.HIGHEST
            )
            update_terms = update_terms * weights[:, None, None]
            partial_blocks = partial_blocks.at[block_row].add(update_terms)
    return jnp.concatenate(pieces_out, axis=0)


def split(values):
    high = values.astype(jnp.bfloat16)
    low = (values - high.astype(jnp.float32)).astype(jnp.bfloat16)
    return high, low


def dot_nt(left, right):
    return lax.dot_general(
        left, right, (((1,), (1,)), ((), ())), preferred_element_type=jnp.float32
    )


def kernel(
    ns,
    nc,
    parent_s,
    order_s,
    col_s,
    rhs_ref,
    row_v,
    col_v,
    inv_hbm,
    fac_hbm,
    out_hbm,
    *scratch,
):
    layout = level_layout()
    names = iter(scratch)
    inv_f, inv_h, inv_l, fac_f, fac_w, upd, sel, solved, out_v = [next(names) for _ in range(9)]
    buffers = {}
    for name, skip in BUFFERS:
        buffers[name] = [None] * skip + [next(names) for _ in layout[skip:]]
    load_sem, store_sem = next(names), next(names)
    x_send, x_recv, a_send, a_recv, b_send, b_recv, s_send, s_recv, c_send, c_recv, d_send, d_recv = [
        next(names) for _ in range(12)
    ]

    r = lax.axis_index("sn")
    c = lax.axis_index("rhs")
    nz, nx = nc, ns // nc
    z = r // nx
    x = r % nx
    active = c <= z
    above = z < nz - 1
    below = z > 0
    beside = r + 1 - 2 * x
    slots = fac_f.shape[0]
    sc = rhs_ref.shape[1]
    rows_s = rhs_ref.shape[2]
    hb = rows_s // BS
    low_nodes = layout[0][1]
    total = inv_f.shape[0]

    barrier = pltpu.get_barrier_semaphore()
    partners = [(lax.rem(r + d, ns), c) for d in range(1, ns)]
    for dx in range(nx):
        for dc in range(1, nc):
            partners.append((z * nx + lax.rem(x + dx, nx), lax.rem(c + dc, nc)))
    for partner in partners:
        pl.semaphore_signal(
            barrier, inc=1, device_id=partner, device_id_type=pl.DeviceIdType.MESH
        )

    load_a = pltpu.make_async_copy(
        inv_hbm.at[pl.ds(0, low_nodes)], inv_f.at[pl.ds(0, low_nodes)], load_sem.at[0]
    )
    load_b = pltpu.make_async_copy(
        inv_hbm.at[pl.ds(low_nodes, total - low_nodes)],
        inv_f.at[pl.ds(low_nodes, total - low_nodes)],
        load_sem.at[1],
    )
    load_c = pltpu.make_async_copy(fac_hbm, fac_f, load_sem.at[2])
    load_a.start()
    load_c.start()
    load_b.start()

    def live_rows(node, h):
        lanes = lax.broadcasted_iota(jnp.int32, (sc, BS), 1) + (r * rows_s + h * BS)
        return lanes < order_s[node]

    def copy(src, dst, ssem, rsem, dev):
        return pltpu.make_async_remote_copy(
            src_ref=src,
            dst_ref=dst,
            send_sem=ssem,
            recv_sem=rsem,
            device_id=dev,
            device_id_type=pl.DeviceIdType.MESH,
        )

    def guard(cond, go):
        go() if cond is None else pl.when(cond)(go)

    def both_of(first_cond, second_cond):
        if first_cond is None:
            return second_cond
        return first_cond if second_cond is None else first_cond & second_cond

    def send(cond, src, dst, ssem, rsem, dev):
        guard(cond, lambda: copy(src, dst, ssem, rsem, dev).start())

    def arrived(cond, piece, sem):
        guard(cond, lambda: copy(piece, piece, sem, sem, (r, c)).wait_recv())

    def landed(cond, count, sem):
        arrived(cond, solved.at[pl.ds(0, count)], sem)

    waits = []

    def sent(cond, count, sem):
        def go():
            piece = solved.at[pl.ds(0, count)]
            copy(piece, piece, sem, sem, (r, c)).wait_send()

        waits.append((cond, go))

    def drain():
        for cond, go in waits:
            guard(cond, go)
        waits.clear()

    stores = []

    def run(level):
        first, members = layout[level]
        mh = members * hb
        base = first * NB
        pieces = PIECES[level]
        nodes = members // pieces
        size = nodes * hb
        own, relay, held, stage, terms, part, got, cross = [
            buffers[name][level]
            for name in ("own", "relay", "held", "stage", "terms", "part", "got", "cross")
        ]
        last = level == LEVELS - 1
        fine = pieces * SUB[level]
        fsize = size // SUB[level]

        def rows(ch):
            return pl.ds(ch * size, size)

        def fine_rows(ch):
            return pl.ds(ch * fsize, fsize)

        def share(ch, to_z, to_x):
            return part.at[pl.ds(((ch * nx + to_x) * nz + to_z) * fsize, fsize)]

        def cross_send(ch):
            if TWO_STEP[level][ch]:
                send(
                    None,
                    part.at[pl.ds((ch * nx + 1 - x) * nz * fsize, nz * fsize)],
                    cross.at[ch],
                    x_send.at[ch],
                    x_recv.at[ch],
                    (beside, c),
                )
                sent(None, nz * fsize, x_send.at[ch])
                return
            for d in range(1, ns):
                to = lax.rem(r + d, ns)
                send(
                    None,
                    share(ch, to // nx, to % nx),
                    got.at[ch, d - 1],
                    a_send.at[ch],
                    a_recv.at[ch],
                    (to, c),
                )
            sent(None, (ns - 1) * fsize, a_send.at[ch])

        def cross_sum(ch):
            if not TWO_STEP[level][ch]:
                return
            arrived(None, cross.at[ch], x_recv.at[ch])

            @pl.loop(0, nz * fsize)
            def _(i):
                spot = (ch * nx + x) * nz * fsize + i
                part[spot] = part[spot] + cross[ch, i]

            for d in range(1, nz):
                to = lax.rem(z + d, nz)
                send(
                    None,
                    share(ch, to, x),
                    got.at[ch, d - 1],
                    a_send.at[ch],
                    a_recv.at[ch],
                    (to * nx + x, c),
                )
            sent(None, (nz - 1) * fsize, a_send.at[ch])

        def own_rows(ch):
            others = nz - 1 if level and TWO_STEP[level][ch] else ns - 1
            if level:
                arrived(None, got.at[ch, pl.ds(0, others)], a_recv.at[ch])

            def one_row(i, node, h):
                value = rhs_ref[node, :, h * BS : (h + 1) * BS]
                if level:
                    value = value - part[((ch * nx + x) * nz + z) * fsize + i]
                    for d in range(others):
                        value = value - got[ch, d, i]
                own[ch * fsize + i] = jnp.where(live_rows(node, h), value, 0.0)

            if fsize < hb:
                one_row(0, first + ch // hb, ch % hb)
                return

            @pl.loop(0, nodes)
            def _(n):
                for h in range(hb):
                    one_row(n * hb + h, first + ch * nodes + n, h)

        def spread(cond, zs, source, ch):
            slot = x * nc + c
            for way, to in ((1, beside), (0, r)):
                send(
                    both_of(cond, c != zs) if way == 0 else cond,
                    source.at[fine_rows(ch)],
                    held.at[slot, fine_rows(ch)],
                    s_send.at[ch],
                    s_recv.at[ch],
                    (to, zs),
                )

            @pl.when(both_of(cond, c == zs))
            def _():
                @pl.loop(ch * fsize, (ch + 1) * fsize)
                def _(i):
                    held[slot, i] = source[i]

        def climb(cond, zs, source, ch, d):
            send(
                both_of(cond, z + d < nz),
                source.at[fine_rows(ch)],
                relay.at[zs, fine_rows(ch)],
                b_send.at[ch],
                b_recv.at[ch, zs],
                (r + nx * d, c),
            )

        def start_rows(ch):
            for d in range(1, 2 if CHAIN[level][ch] else nz):
                climb(None, z, own, ch, d)
            if level:
                spread(None, z, own, ch)
            for t in range(nz):
                climbs = (t + 1 if t < nz - 1 else 0) if CHAIN[level][ch] else nz - 1 - t
                if climbs:
                    sent(z == t, climbs * fsize, b_send.at[ch])
                sent((z == t) & active, (2 * t + 1) * fsize, s_send.at[ch])
                if t < nz - 1:
                    sent((z == t) & (c > z), (2 * t + 2) * fsize, s_send.at[ch])

        def pass_rows(ch):
            for d in range(1, nz):
                zs = jnp.maximum(z - d, 0)
                arrived(z >= d, relay.at[zs, fine_rows(ch)], b_recv.at[ch, zs])
                if CHAIN[level][ch]:
                    climb(z >= d, zs, relay.at[zs], ch, 1)
                spread(z >= d, zs, relay.at[zs], ch)
            if level == 0:
                spread(None, z, own, ch)

        def product(ch):
            for f in range(ch * SUB[level], (ch + 1) * SUB[level]):
                landed(active, (ns - 1) * fsize, s_recv.at[f])

            @pl.when(active)
            def _():
                @pl.loop(ch * nodes, (ch + 1) * nodes)
                def _(n):
                    columns = []
                    for qi in range(nx):
                        for h in range(hb):
                            columns.append(
                                jnp.concatenate(
                                    [held[qi * nc + c2, n * hb + h] for c2 in range(nc)], axis=0
                                )
                            )
                    high, low = split(jnp.concatenate(columns, axis=1))
                    right_h = inv_h[first + n]
                    right_l = inv_l[first + n]
                    value = dot_nt(high, right_h) + (dot_nt(low, right_h) + dot_nt(high, right_l))
                    for c2 in range(nc):
                        for h in range(hb):
                            stage[c2, n * hb + h] = value[
                                c2 * sc : (c2 + 1) * sc, h * BS : (h + 1) * BS
                            ]
                    for h in range(hb):
                        terms[c, n * hb + h] = stage[c, n * hb + h]

            for d in range(1, nc):
                to = lax.rem(c + d, nc)
                send(
                    active,
                    stage.at[to, rows(ch)],
                    terms.at[c, rows(ch)],
                    c_send.at[ch],
                    c_recv.at[ch],
                    (r, to),
                )
            sent(active, (nc - 1) * size, c_send.at[ch])

        def rows_of(rs, ch):
            return solved.at[pl.ds(base + rs * mh + ch * size, size)]

        def gather(cond, rs, ch, to, place=None):
            place = rs // nx if place is None else place
            send(
                cond,
                rows_of(rs, ch),
                rows_of(rs, ch),
                d_send.at[ch],
                d_recv.at[ch, place],
                (to, c),
            )

        def collect(ch):
            for t in range(nz):
                if t:
                    landed((z == t) & active, t * size, c_recv.at[ch])
                if t < nz - 1:
                    landed((z == t) & (c > z), (t + 1) * size, c_recv.at[ch])
            for t in range(nz):

                @pl.when(z == t)
                def _(t=t):
                    @pl.loop(ch * nodes, (ch + 1) * nodes)
                    def _(n):
                        for h in range(hb):
                            i = n * hb + h
                            value = terms[0, i]
                            for c2 in range(1, t + 1):
                                value = value + terms[c2, i]
                            value = jnp.where(live_rows(first + n, h), value, 0.0)
                            out_v[first + n, :, h * BS : (h + 1) * BS] = value
                            if not last:
                                solved[base + r * mh + i] = value

            if last:
                return
            if CHAIN_BACK[level][ch]:
                gather(above, r, ch, r + nx)
                gather(below, r, ch, r - nx)
            else:
                for d in range(1, nz):
                    gather(None, r, ch, lax.rem(z + d, nz) * nx + x)
            gather(None, r, ch, beside, nz)

        def pass_one(ch, step, d, cond=None):
            there = both_of(cond, z >= d if step < 0 else z + d < nz)
            rs = r + step * d * nx
            arrived(there, rows_of(rs, ch), d_recv.at[ch, rs // nx])
            if CHAIN_BACK[level][ch]:
                gather(there & (above if step < 0 else below), rs, ch, r - step * nx)
            gather(there, rs, ch, beside, nz)

        def pass_lower(ch):
            for d in range(1, nz):
                pass_one(ch, -1, d)

        early = range(2 if pieces > 2 else 0)

        def pass_early(ch):
            if ch in early:
                pass_one(ch, 1, 1, z == nz - 2)

        def pass_upper():
            order = [(2 * ch + LAG * (d - 1), d, ch) for ch in range(pieces) for d in range(1, nz)]
            for _, d, ch in sorted(order):
                pass_one(ch, 1, d, z < nz - 2 if d == 1 and ch in early else None)
            for ch in range(pieces):
                if CHAIN_BACK[level][ch]:
                    sent(above & below, (2 * nz + 1) * size, d_send.at[ch])
                    sent((z == 0) | (z == nz - 1), (nz + 1) * size, d_send.at[ch])
                else:
                    sent(None, (2 * nz - 1) * size, d_send.at[ch])

        stages = [own_rows_and_start(own_rows, start_rows), pass_rows, product, collect]
        if level:
            for ch in range(fine):
                cross_send(ch)
            stages.insert(0, cross_sum)
        else:
            for ch in range(pieces):
                own_rows(ch)
                if ch == 0:
                    pl.semaphore_wait(barrier, len(partners))
                start_rows(ch)
            stages.pop(0)
        if not last:
            stages.append(pass_lower)
        whole = (product, collect, pass_lower)
        for t in range(fine + len(stages) - 1):
            if level == 0 and t == 0:

                @pl.loop(low_nodes * NB, solved.shape[0])
                def _(index):
                    solved[index] = jnp.zeros((sc, BS), jnp.float32)

                load_a.wait()

                @pl.when(active)
                def _():
                    split_inverse(inv_f, inv_h, inv_l, 0, low_nodes)

            if level == 0 and t == 1:
                make_selection(parent_s, row_v, col_v, sel, layout, hb, ns // nc, nc)
                load_c.wait()
                load_b.wait()

                @pl.when(active)
                def _():
                    split_inverse(inv_f, inv_h, inv_l, low_nodes, total)

            passed = t - stages.index(collect)
            if passed == 2:
                pass_early(0)
            for s, one in enumerate(stages):
                count = SUB[level] if one in whole else 1
                step = t - s + 1
                if step % count == 0 and 0 < step <= fine:
                    one(step // count - 1)
            if passed == 3:
                pass_early(1)
        if level == 0:
            turn_blocks(z == 0)
        if not last:
            pass_upper()
        if level == 0:
            turn_blocks(z > 0)
        store = pltpu.make_async_copy(
            out_v.at[pl.ds(first, members)],
            out_hbm.at[pl.ds(first, members)],
            store_sem.at[level],
        )
        store.start()
        stores.append(store)
        if not last:
            for ch in range(pieces):
                landed(None, nz * size, d_recv.at[ch, nz])

    def turn_blocks(cond):
        @pl.when(cond)
        def _():
            @pl.loop(0, slots, unroll=4)
            def _(k):
                high, low = split(jnp.transpose(fac_f[k]))
                fac_w[k, 0:BS, :] = high
                fac_w[k, BS : 2 * BS, :] = low

    def update(level):
        first, members = layout[level]
        part = buffers["part"][level]

        def one_block(k, carry):
            block = col_s[k]
            node = block // NB
            inside = block % NB
            offset = jnp.int32(0)
            count = jnp.int32(layout[0][1])
            for begin, many in layout[1:-1]:
                over = node >= begin
                offset = jnp.where(over, begin, offset)
                count = jnp.where(over, many, count)
            index = (
                offset * NB
                + (inside // hb) * (count * hb)
                + (node - offset) * hb
                + inside % hb
            )
            high, low = split(solved[index])
            left = jnp.concatenate(
                [
                    jnp.concatenate([high, high], axis=1),
                    jnp.concatenate([low, jnp.zeros_like(low)], axis=1),
                ],
                axis=0,
            )
            both = jnp.dot(left, fac_w[k], preferred_element_type=jnp.float32)
            upd[pl.ds(pl.multiple_of(k * sc, sc), sc), :] = both[:sc] + both[sc:]
            return carry

        lax.fori_loop(0, slots, one_block, 0, unroll=slots // 2)

        sel_first = (first - low_nodes) * NB
        picked = sel[sel_first : sel_first + members * NB, :]
        for s in range(0, sc, 2):
            pair = jnp.concatenate(
                [upd[pl.ds(s + t, slots, stride=sc), :] for t in range(2)], axis=1
            )
            summed = jnp.dot(
                picked,
                jnp.concatenate(split(pair), axis=0),
                preferred_element_type=jnp.float32,
            )
            for t in range(2):
                part.reshape(members * NB * sc, BS)[
                    pl.ds(s + t, members * NB, stride=sc), :
                ] = summed[:, t * BS : (t + 1) * BS]

    for level in range(LEVELS):
        if level:
            update(level)
            drain()
        run(level)
    for store in stores:
        store.wait()
    drain()


def own_rows_and_start(own_rows, start_rows):
    def go(ch):
        own_rows(ch)
        start_rows(ch)

    return go


def split_inverse(inv_f, inv_h, inv_l, begin, stop):
    chunk = 32
    rows = inv_f.shape[1]

    @pl.loop(begin, stop)
    def _(n):
        @pl.loop(0, rows // chunk)
        def _(i):
            part = pl.ds(pl.multiple_of(i * chunk, chunk), chunk)
            high, low = split(inv_f[n, part, :])
            inv_h[n, part, :] = high
            inv_l[n, part, :] = low


def make_selection(parent_s, row_v, col_v, sel, layout, hb, nx, nz):
    row_block = row_v[...]
    row_node = row_block // NB
    walker = col_v[...] // NB
    valid = jnp.zeros(walker.shape, jnp.bool_)
    nodes = layout[-1][0] + 1
    for repeat in range(LEVELS - 1):
        moved = jnp.zeros_like(walker)
        for t in range(nodes):
            moved = jnp.where(walker == t, parent_s[t], moved)
        walker = moved
        valid = valid | (walker == row_node)
    inside = row_block % NB
    place = jnp.full(row_block.shape, -1, jnp.int32)
    low_nodes = layout[0][1]
    holder = inside // hb
    for level in range(1, LEVELS):
        begin, many = layout[level]
        nodes = many // PIECES[level]
        chunk = (row_node - begin) // nodes
        spot = (
            (begin - low_nodes) * NB
            + ((chunk * nx + holder % nx) * nz + holder // nx) * (nodes * hb)
            + (row_node - begin - chunk * nodes) * hb
            + inside % hb
        )
        if SUB[level] > 1:
            chunk = (row_node - begin) * hb + inside % hb
            spot = (begin - low_nodes) * NB + (chunk * nx + holder % nx) * nz + holder // nx
        place = jnp.where(row_node >= begin, spot, place)
    place = jnp.where(valid, place, -1)
    count, slots = sel.shape[0], row_block.shape[1]
    rows = lax.broadcasted_iota(jnp.int32, (count, slots), 0)
    hits = rows == jnp.broadcast_to(place, (count, slots))
    once = jnp.where(hits, 1.0, 0.0).astype(jnp.bfloat16)
    sel[...] = jnp.concatenate([once, once], axis=1)


def fused_device(
    ns, nc, right_side, inverse_diag, factor_blocks, parent, node_order, block_row, block_col
):
    total, sc, rows_s = right_side.shape
    columns = inverse_diag.shape[2]
    slots = factor_blocks.shape[0]
    hb = rows_s // BS
    layout = level_layout()
    f32, bf16 = jnp.float32, jnp.bfloat16
    upper = total - layout[0][1]


    def per_level(lead, skip=0):
        return [pltpu.VMEM((*lead, m * hb, sc, BS), f32) for _, m in layout[skip:]]

    def per_piece(lead):
        return [
            pltpu.VMEM(
                (PIECES[k] * SUB[k], *lead(k, layout[k][1] * hb // PIECES[k] // SUB[k]), sc, BS), f32
            )
            for k in range(1, LEVELS)
        ]

    sems = pltpu.SemaphoreType.DMA
    most = max(count * sub for count, sub in zip(PIECES, SUB))
    scratch = [
        pltpu.VMEM((total, rows_s, columns), f32),
        pltpu.VMEM((total, rows_s, columns), bf16),
        pltpu.VMEM((total, rows_s, columns), bf16),
        pltpu.VMEM((slots, BS, BS), f32),
        pltpu.VMEM((slots, 2 * BS, BS), bf16),
        pltpu.VMEM((slots * sc, BS), f32),
        pltpu.VMEM((upper * NB, 2 * slots), bf16),
        pltpu.VMEM(((total - 1) * NB, sc, BS), f32),
        pltpu.VMEM(right_side.shape, f32),
        *per_level(()),
        *per_level((nc - 1,)),
        *per_level((ns,)),
        *per_level((nc,)),
        *per_level((nc,)),
        *[pltpu.VMEM((m * NB, sc, BS), f32) for _, m in layout[1:]],
        *per_piece(lambda k, size: (ns - 1, size)),
        *per_piece(lambda k, size: (nc * size,)),
        sems((3,)),
        sems((LEVELS,)),
        sems((most,)),
        sems((most,)),
        sems((most,)),
        sems((most,)),
        sems((most,)),
        sems((most, nc - 1)),
        sems((most,)),
        sems((most,)),
        sems((most,)),
        sems((most,)),
        sems((most,)),
        sems((most, nc + 1)),
    ]
    smem = pl.BlockSpec(memory_space=pltpu.SMEM)
    vmem = pl.BlockSpec(memory_space=pltpu.VMEM)
    hbm = pl.BlockSpec(memory_space=pl.ANY)
    return pl.pallas_call(
        functools.partial(kernel, ns, nc),
        out_shape=jax.ShapeDtypeStruct(right_side.shape, f32),
        in_specs=[smem, smem, smem, vmem, vmem, vmem, hbm, hbm],
        out_specs=hbm,
        scratch_shapes=scratch,
        compiler_params=pltpu.CompilerParams(
            collective_id=0, has_side_effects=True, vmem_limit_bytes=60 * 2**20
        ),
        name="substitute",
    )(
        parent,
        node_order,
        block_col,
        right_side,
        block_row[None, :],
        block_col[None, :],
        inverse_diag,
        factor_blocks,
    )


def solution(mesh):
    ns, nc = mesh.shape["sn"], mesh.shape["rhs"]
    in_specs = (
        P(None, "rhs", "sn"),
        P(None, "sn", "rhs"),
        P("sn", None, None),
        P(),
        P(),
        P("sn"),
        P("sn"),
    )
    out_specs = P(None, "rhs", "sn")
    fused = S == 2 * BS * ns and ns == 2 * nc and nc == 4
    body = functools.partial(fused_device, ns, nc) if fused else per_device
    return jax.shard_map(
        body, mesh=mesh, in_specs=in_specs, out_specs=out_specs, check_vma=False
    )
```
